768 devices in a mesh: ctx: 12 (over z), head: 64 (over y, x, core).
Axes of the slice: x: 4, y: 8, z: 12, core: 2. Of those that a mesh axis runs over, the one named last changes fastest.
Arguments:
- incoming_signals: bfloat16 [6144, 4096], P('ctx'), may hold values from -6 to 6
- receptor_linear_map: bfloat16 [4096, 4096], P(None, 'head'), may hold values from -0.09375 to 0.09375
- lock_linear_map: bfloat16 [4096, 4096], P(None, 'head'), may hold values from -0.09375 to 0.09375
- worth_linear_map: bfloat16 [4096, 4096], P(None, 'head'), may hold values from -0.09375 to 0.09375
- outbound_linear_map: bfloat16 [4096, 4096], P('head'), may hold values from -0.25 to 0.25
- selfward_extra: float32 [4096], P('head'), may hold values from 2 to 32
- cluster_amplify_level: float32 [4096], P('head'), may hold values from 0.25 to 1.75
- dwindle_powers: int32 [4096], P('head'), may hold values from 0 to 63
- bisect_indicators: int32 [6144], P('ctx'), may hold values 0 or 1
- tutor_aggregated: bfloat16 [6144, 4096], P('ctx', 'head'), may hold values from -6 to 6
Outputs:
- mixed: bfloat16 [6144, 4096], P('ctx', 'head')
- receptor_sensitivity: bfloat16 [6144, 4096], P('ctx', 'head')
- grad_keys: bfloat16 [6144, 4096], P('ctx', 'head')
- value_gradients: bfloat16 [6144, 4096], P('ctx', 'head')
The draws below stay inside these ranges and needn't reach their ends.
All inputs are finite; a program needn't handle non-finite values. No bound on the sum of `bisect_indicators` on one device may be relied on, other than what follows from the above.
Results may differ from the reference program's by a relative error of at most 0.014.
Values may be sent and summed in bfloat16 or wider, within the bound.
No kernel may reach another device: no remote copies, remote signals or barrier semaphores. Data moves between devices by JAX's collectives and lax.ppermute only.
A program may use at most 64 MiB of HBM per device.

```python
import math
import jax
import jax.numpy as jnp
from jax import lax

LANES_EACH_HEAD = 64
HIDDEN_BREADTH = 4096
TOK_DEV = 512
FRAMES = 6144
CODES = 64
N_CTX = 12


def touch_ends(values, rng, least, high):
    shape = values.shape
    place = [jax.random.randint(jax.random.fold_in(rng, axis), (), 0, shape[axis]) for axis in range(len(shape))]
    values = values.at[tuple(place)].set(least)
    longest = shape.index(max(shape))
    place[longest] = (place[longest] + 1) % shape[longest]
    return values.at[tuple(place)].set(high)


def strengthened(values, stream_key, source, target, parts, factor):
    owner, partner = [(jnp.arange(values.shape[axis_at]) // (values.shape[axis_at] // parts)).reshape([-1 if axis == axis_at else 1 for axis in range(values.ndim)]) for axis_at in (source, target)]
    chosen = jax.random.permutation(stream_key, parts)[partner]
    strong = (owner == chosen) | (owner == (partner + parts // 2) % parts)
    return jnp.where(strong, factor * values, values)


def block_levels(rng, dims, cuts, smallest, high):
    factor_of = 1.0
    for position, blocks in cuts:
        heights = jax.random.uniform(jax.random.fold_in(jax.random.fold_in(rng, 6), position), (blocks,), jnp.float32, smallest / len(cuts), high / len(cuts))
        factor_of = factor_of * jnp.repeat(jnp.exp(heights), dims[position] // blocks).reshape((-1,) + (1,) * (len(dims) - 1 - position))
    return factor_of


def scatter_about(stream_key, shape, spread, bound, split=(), kind=jnp.bfloat16):
    entries = spread * jax.random.normal(stream_key, shape, jnp.float32)
    if split:
        entries = entries * block_levels(stream_key, shape, split, -0.22, 0.18)
    return jnp.clip(entries, -bound, bound).astype(kind)


def noise_with(key, dims, width, reach, pieces, heavy, dtype=jnp.bfloat16):
    result = width * jax.random.normal(key, dims, jnp.float32)
    if pieces:
        result = result * block_levels(key, dims, pieces, -0.22, 0.18)
    return jnp.clip(strengthened(result, jax.random.fold_in(key, 3), *heavy), -reach, reach).astype(dtype)


def setup_inputs(seed: int = 0) -> dict:
    streams_of = jax.random.split(jax.random.key(seed), 11)
    incoming_signals = scatter_about(streams_of[0], (FRAMES, HIDDEN_BREADTH), 1.0, 6.0, ((0, 12),))
    receptor_linear_map = scatter_about(streams_of[1], (HIDDEN_BREADTH, HIDDEN_BREADTH), HIDDEN_BREADTH ** -0.5, 0.09375, ((1, 64),))
    lock_linear_map = scatter_about(streams_of[2], (HIDDEN_BREADTH, HIDDEN_BREADTH), HIDDEN_BREADTH ** -0.5, 0.09375, ((1, 64),))
    worth_linear_map = scatter_about(streams_of[3], (HIDDEN_BREADTH, HIDDEN_BREADTH), HIDDEN_BREADTH ** -0.5, 0.09375, ((1, 64),))
    outbound_linear_map = noise_with(streams_of[4], (HIDDEN_BREADTH, HIDDEN_BREADTH), HIDDEN_BREADTH ** -0.5, 0.25, ((0, 64),), (0, 1, 64, 4.0))
    selfward_extra = jnp.clip(jnp.exp(math.log(32.0) - 2.7725887 * jax.random.uniform(streams_of[5], (HIDDEN_BREADTH,), jnp.float32) ** block_levels(streams_of[5], (HIDDEN_BREADTH,), ((0, 64),), -0.2, 0.2)), 2.0, 32.0)
    cluster_amplify_level = jnp.clip(1.0 + 0.15 * jax.random.normal(streams_of[6], (HIDDEN_BREADTH,), jnp.float32), 0.25, 1.75)
    dwindle_powers = touch_ends(jax.random.randint(streams_of[7], (HIDDEN_BREADTH,), 0, CODES), jax.random.fold_in(streams_of[7], 1), 0, CODES - 1).astype(jnp.int32)
    bisect_indicators = touch_ends((jax.random.randint(streams_of[8], (FRAMES,), 0, FRAMES) < 4).astype(jnp.int32), jax.random.fold_in(streams_of[8], 1), 0, 1)
    tutor_aggregated = scatter_about(streams_of[9], (FRAMES, HIDDEN_BREADTH), 1.0, 6.0, ((0, 12), (1, 64)))
    return {"incoming_signals": incoming_signals, "receptor_linear_map": receptor_linear_map, "lock_linear_map": lock_linear_map, "worth_linear_map": worth_linear_map, "outbound_linear_map": outbound_linear_map, "selfward_extra": selfward_extra, "cluster_amplify_level": cluster_amplify_level, "dwindle_powers": dwindle_powers, "bisect_indicators": bisect_indicators, "tutor_aggregated": tutor_aggregated}


numeric_fidelity = lax.Precision.HIGHEST
epsilon = 1e-05
log_half = -0.6931471805599453
rate_span = 1.2

def key_norm(keys_raw):
    scale = lax.rsqrt(lax.optimization_barrier(jnp.mean(keys_raw * keys_raw, axis=-1, keepdims=True)) + epsilon)
    return (keys_raw * scale * 0.125, scale)

def key_norm_back(keys_raw, scale, sensitivity_whitened_guess):
    inner = lax.optimization_barrier(jnp.mean(keys_raw * sensitivity_whitened_guess, axis=-1, keepdims=True))
    return 0.125 * scale * (sensitivity_whitened_guess - scale * scale * keys_raw * inner)

def head_norm(generated_elements):
    centred = generated_elements - lax.optimization_barrier(jnp.mean(generated_elements, axis=-1, keepdims=True))
    inverse = lax.rsqrt(lax.optimization_barrier(jnp.mean(centred * centred, axis=-1, keepdims=True)) + epsilon)
    return (centred * inverse, inverse)

def head_norm_back(unit, inverse, gain, grad_normed):
    scaled = grad_normed * gain
    return inverse * (scaled - lax.optimization_barrier(jnp.mean(scaled, axis=-1, keepdims=True)) - unit * lax.optimization_barrier(jnp.mean(scaled * unit, axis=-1, keepdims=True)))

def piece_summands(receptor_linear_coeffs, lock_linear_coeffs, prefix_logarithm):
    length = prefix_logarithm.shape[1]
    last = prefix_logarithm[:, length - 1:, :]
    enlarging_quotient = jnp.exp(prefix_logarithm)
    dwindling_quotient = jnp.exp(-prefix_logarithm)
    inquiry_this_moment = receptor_linear_coeffs * enlarging_quotient
    lock_this_moment = lock_linear_coeffs * dwindling_quotient
    closing_addition = jnp.exp(last - prefix_logarithm)
    forgetting_rate = jnp.exp(last[:, 0, :])
    triangular_mask = jnp.arange(length)[:, None] >= jnp.arange(length)[None, :]
    affinity_logits = jnp.where(triangular_mask[None], jnp.einsum('htk,hsk->hts', inquiry_this_moment, lock_this_moment, precision=numeric_fidelity), 0.0)
    return (enlarging_quotient, dwindling_quotient, inquiry_this_moment, lock_this_moment, closing_addition, forgetting_rate, triangular_mask, affinity_logits)

def slice_yields(receptor_linear_coeffs, lock_linear_coeffs, worth_linear_coeffs, selfward_extra, collated_additions, beginning_hidden_carryover):
    instant_portion_amount = lax.optimization_barrier(jnp.sum(receptor_linear_coeffs * selfward_extra * lock_linear_coeffs, axis=-1, keepdims=True))
    return jnp.einsum('how,hwr->hor', collated_additions[7], worth_linear_coeffs, precision=numeric_fidelity) + jnp.einsum('kdo,kom->kdm', collated_additions[2], beginning_hidden_carryover, precision=numeric_fidelity) + instant_portion_amount * worth_linear_coeffs

def slice_sensitivities(receptor_linear_coeffs, lock_linear_coeffs, worth_linear_coeffs, selfward_extra, collated_additions, beginning_hidden_carryover, walking_hidden_carryover, outcome_sensitivity):
    enlarging_quotient, dwindling_quotient, inquiry_this_moment, lock_this_moment, closing_addition, forgetting_rate, triangular_mask, affinity_logits = collated_additions
    twofold_contracted_mul = jnp.where(triangular_mask[None], jnp.einsum('htv,hsv->hts', outcome_sensitivity, worth_linear_coeffs, precision=numeric_fidelity), 0.0)
    progressive_totals = lax.optimization_barrier(jnp.sum(outcome_sensitivity * worth_linear_coeffs, axis=-1, keepdims=True))
    instant_portion_amount = lax.optimization_barrier(jnp.sum(receptor_linear_coeffs * selfward_extra * lock_linear_coeffs, axis=-1, keepdims=True))
    receptor_sensitivity = enlarging_quotient * (jnp.einsum('kvn,kgn->kvg', outcome_sensitivity, beginning_hidden_carryover, precision=numeric_fidelity) + jnp.einsum('bnd,bdf->bnf', twofold_contracted_mul, lock_this_moment, precision=numeric_fidelity)) + progressive_totals * selfward_extra * lock_linear_coeffs
    sensitivity_whitened_guess = dwindling_quotient * jnp.einsum('zwh,zws->zhs', twofold_contracted_mul, inquiry_this_moment, precision=numeric_fidelity) + closing_addition * jnp.einsum('kop,kup->kou', worth_linear_coeffs, walking_hidden_carryover, precision=numeric_fidelity) + progressive_totals * selfward_extra * receptor_linear_coeffs
    value_gradients = jnp.einsum('ljp,lje->lpe', affinity_logits, outcome_sensitivity, precision=numeric_fidelity) + jnp.einsum('ely,eyc->elc', lock_linear_coeffs * closing_addition, walking_hidden_carryover, precision=numeric_fidelity) + instant_portion_amount * outcome_sensitivity
    return (receptor_sensitivity, sensitivity_whitened_guess, value_gradients)

def reference(incoming_signals, receptor_linear_map, lock_linear_map, worth_linear_map, outbound_linear_map, selfward_extra, cluster_amplify_level, dwindle_powers, bisect_indicators, tutor_aggregated):
    cluster_number_series = HIDDEN_BREADTH // LANES_EACH_HEAD
    blocks = N_CTX
    length = TOK_DEV

    def by_head(array):
        return array.reshape(blocks, length, cluster_number_series, LANES_EACH_HEAD).transpose(0, 2, 1, 3)

    def by_frame(array):
        return array.transpose(0, 2, 1, 3).reshape(blocks * length, cluster_number_series * LANES_EACH_HEAD)
    receptor_linear_coeffs = by_head(jnp.dot(incoming_signals, receptor_linear_map, preferred_element_type=jnp.float32))
    keys_raw = by_head(jnp.dot(incoming_signals, lock_linear_map, preferred_element_type=jnp.float32))
    worth_linear_coeffs = by_head(jnp.dot(incoming_signals, worth_linear_map, preferred_element_type=jnp.float32))
    lock_linear_coeffs, scale = key_norm(keys_raw)
    rate = -rate_span * (dwindle_powers.astype(jnp.float32) + 1.0) / float(CODES * FRAMES)
    log_steps = rate.reshape(1, cluster_number_series, 1, LANES_EACH_HEAD) + (bisect_indicators.astype(jnp.float32) * log_half).reshape(blocks, 1, length, 1)
    prefix_logarithm = jnp.cumsum(log_steps, axis=2)
    stacked_selfward_extras = selfward_extra.reshape(cluster_number_series, 1, LANES_EACH_HEAD)
    gain_heads = cluster_amplify_level.reshape(cluster_number_series, 1, LANES_EACH_HEAD)
    zero_state = jnp.zeros((cluster_number_series, LANES_EACH_HEAD, LANES_EACH_HEAD), jnp.float32)

    def forward_block(changing_hidden_carryover, item):
        span_receptor_valves, span_lock_arrays, span_worth_arrays, prefix_piece_logs = item
        collated_additions = piece_summands(span_receptor_valves, span_lock_arrays, prefix_piece_logs)
        generated_elements = slice_yields(span_receptor_valves, span_lock_arrays, span_worth_arrays, stacked_selfward_extras, collated_additions, changing_hidden_carryover)
        within_piece_share = jnp.einsum('atn,ato->ano', span_lock_arrays * collated_additions[4], span_worth_arrays, precision=numeric_fidelity)
        return (collated_additions[5][..., None] * changing_hidden_carryover + within_piece_share, (generated_elements, changing_hidden_carryover))
    unused, (generated_elements, starts) = lax.scan(forward_block, zero_state, (receptor_linear_coeffs, lock_linear_coeffs, worth_linear_coeffs, prefix_logarithm))
    unit, inverse = head_norm(generated_elements)
    normed = by_frame(unit * gain_heads).astype(jnp.bfloat16)
    mixed = jnp.dot(normed, outbound_linear_map, preferred_element_type=jnp.float32).astype(jnp.bfloat16)
    diff = (mixed.astype(jnp.float32) - tutor_aggregated.astype(jnp.float32)).astype(jnp.bfloat16)
    grad_normed = by_head(jnp.dot(diff, outbound_linear_map.T, preferred_element_type=jnp.float32))
    outcome_sensitivity = head_norm_back(unit, inverse, gain_heads, grad_normed)

    def backward_block(walking_hidden_carryover, item):
        span_receptor_valves, span_lock_arrays, span_worth_arrays, prefix_piece_logs, span_inbound_cache, span_sensitivities = item
        collated_additions = piece_summands(span_receptor_valves, span_lock_arrays, prefix_piece_logs)
        sensitivity_bundle = slice_sensitivities(span_receptor_valves, span_lock_arrays, span_worth_arrays, stacked_selfward_extras, collated_additions, span_inbound_cache, walking_hidden_carryover, span_sensitivities)
        reverse_sweeping = jnp.einsum('atn,ato->ano', collated_additions[2], span_sensitivities, precision=numeric_fidelity)
        return (collated_additions[5][..., None] * walking_hidden_carryover + reverse_sweeping, sensitivity_bundle)
    unused_carry, (receptor_sensitivity, sensitivity_whitened_guess, value_gradients) = lax.scan(backward_block, zero_state, (receptor_linear_coeffs, lock_linear_coeffs, worth_linear_coeffs, prefix_logarithm, starts, outcome_sensitivity), reverse=True)
    grad_keys = key_norm_back(keys_raw, scale, sensitivity_whitened_guess)
    return (mixed, by_frame(receptor_sensitivity).astype(jnp.bfloat16), by_frame(grad_keys).astype(jnp.bfloat16), by_frame(value_gradients).astype(jnp.bfloat16))
```

```python
import jax
import jax.numpy as jnp
from jax import lax
from jax.sharding import Mesh, PartitionSpec as P

LANES_EACH_HEAD = 64
CODES = 64


numeric_fidelity = lax.Precision.HIGHEST
epsilon = 1e-05
log_half = -0.6931471805599453
rate_span = 1.2


def key_norm(keys_raw):
    scale = lax.rsqrt(jnp.mean(keys_raw * keys_raw, axis=-1, keepdims=True) + epsilon)
    return (keys_raw * scale * 0.125, scale)


def key_norm_back(keys_raw, scale, sensitivity_whitened_guess):
    inner = jnp.mean(keys_raw * sensitivity_whitened_guess, axis=-1, keepdims=True)
    return 0.125 * scale * (sensitivity_whitened_guess - scale * scale * keys_raw * inner)


def head_norm(generated_elements):
    centred = generated_elements - jnp.mean(generated_elements, axis=-1, keepdims=True)
    inverse = lax.rsqrt(jnp.mean(centred * centred, axis=-1, keepdims=True) + epsilon)
    return (centred * inverse, inverse)


def head_norm_back(unit, inverse, gain, grad_normed):
    scaled = grad_normed * gain
    return inverse * (
        scaled
        - jnp.mean(scaled, axis=-1, keepdims=True)
        - unit * jnp.mean(scaled * unit, axis=-1, keepdims=True)
    )


def piece_summands(receptor_linear_coeffs, lock_linear_coeffs, prefix_logarithm):
    length = prefix_logarithm.shape[1]
    last = prefix_logarithm[:, length - 1 :, :]
    enlarging_quotient = jnp.exp(prefix_logarithm)
    dwindling_quotient = jnp.exp(-prefix_logarithm)
    inquiry_this_moment = receptor_linear_coeffs * enlarging_quotient
    lock_this_moment = lock_linear_coeffs * dwindling_quotient
    closing_addition = jnp.exp(last - prefix_logarithm)
    forgetting_rate = jnp.exp(last[:, 0, :])
    triangular_mask = jnp.arange(length)[:, None] >= jnp.arange(length)[None, :]
    affinity_logits = jnp.where(
        triangular_mask[None],
        jnp.einsum(
            "htk,hsk->hts", inquiry_this_moment, lock_this_moment, precision=numeric_fidelity
        ),
        0.0,
    )
    return (
        enlarging_quotient,
        dwindling_quotient,
        inquiry_this_moment,
        lock_this_moment,
        closing_addition,
        forgetting_rate,
        triangular_mask,
        affinity_logits,
    )


def slice_yields(
    receptor_linear_coeffs,
    lock_linear_coeffs,
    worth_linear_coeffs,
    selfward_extra,
    collated_additions,
    beginning_hidden_carryover,
):
    instant_portion_amount = jnp.sum(
        receptor_linear_coeffs * selfward_extra * lock_linear_coeffs, axis=-1, keepdims=True
    )
    return (
        jnp.einsum(
            "how,hwr->hor", collated_additions[7], worth_linear_coeffs, precision=numeric_fidelity
        )
        + jnp.einsum(
            "kdo,kom->kdm",
            collated_additions[2],
            beginning_hidden_carryover,
            precision=numeric_fidelity,
        )
        + instant_portion_amount * worth_linear_coeffs
    )


def slice_sensitivities(
    receptor_linear_coeffs,
    lock_linear_coeffs,
    worth_linear_coeffs,
    selfward_extra,
    collated_additions,
    beginning_hidden_carryover,
    walking_hidden_carryover,
    outcome_sensitivity,
):
    (
        enlarging_quotient,
        dwindling_quotient,
        inquiry_this_moment,
        lock_this_moment,
        closing_addition,
        forgetting_rate,
        triangular_mask,
        affinity_logits,
    ) = collated_additions
    twofold_contracted_mul = jnp.where(
        triangular_mask[None],
        jnp.einsum(
            "htv,hsv->hts", outcome_sensitivity, worth_linear_coeffs, precision=numeric_fidelity
        ),
        0.0,
    )
    progressive_totals = jnp.sum(outcome_sensitivity * worth_linear_coeffs, axis=-1, keepdims=True)
    instant_portion_amount = jnp.sum(
        receptor_linear_coeffs * selfward_extra * lock_linear_coeffs, axis=-1, keepdims=True
    )
    receptor_sensitivity = (
        enlarging_quotient
        * (
            jnp.einsum(
                "kvn,kgn->kvg",
                outcome_sensitivity,
                beginning_hidden_carryover,
                precision=numeric_fidelity,
            )
            + jnp.einsum(
                "bnd,bdf->bnf", twofold_contracted_mul, lock_this_moment, precision=numeric_fidelity
            )
        )
        + progressive_totals * selfward_extra * lock_linear_coeffs
    )
    sensitivity_whitened_guess = (
        dwindling_quotient
        * jnp.einsum(
            "zwh,zws->zhs", twofold_contracted_mul, inquiry_this_moment, precision=numeric_fidelity
        )
        + closing_addition
        * jnp.einsum(
            "kop,kup->kou",
            worth_linear_coeffs,
            walking_hidden_carryover,
            precision=numeric_fidelity,
        )
        + progressive_totals * selfward_extra * receptor_linear_coeffs
    )
    value_gradients = (
        jnp.einsum("ljp,lje->lpe", affinity_logits, outcome_sensitivity, precision=numeric_fidelity)
        + jnp.einsum(
            "ely,eyc->elc",
            lock_linear_coeffs * closing_addition,
            walking_hidden_carryover,
            precision=numeric_fidelity,
        )
        + instant_portion_amount * outcome_sensitivity
    )
    return (receptor_sensitivity, sensitivity_whitened_guess, value_gradients)


GRID = {"y": 8, "x": 4, "core": 2}
TILE = ("x", "core")


def exchange(array, axis):
    return lax.all_to_all(array, axis, 0, 0)


def to_all(array, axis, count):
    return exchange(jnp.broadcast_to(array[None], (count,) + array.shape), axis)


def gather_rows(local):
    n = GRID["x"]
    parts = [local]
    for step in (1, 3, 2):
        parts.append(lax.ppermute(local, "x", [(i, (i + step) % n) for i in range(n)]))
    mine = jnp.concatenate([parts[0], parts[1], parts[3], parts[2]], axis=0)
    return mine, lax.ppermute(mine, "core", [(0, 1), (1, 0)])


def weights_between(log_totals, mine, backward):
    count = log_totals.shape[0]
    at = jnp.arange(count)
    if backward:
        between = (at[None, :] > mine) & (at[None, :] < at[:, None])
        counts = at > mine
    else:
        between = (at[None, :] < mine) & (at[None, :] > at[:, None])
        counts = at < mine
    span = jnp.sum(jnp.where(between[:, :, None], log_totals[None], 0.0), axis=1)
    return jnp.where(counts[:, None], jnp.exp(span), 0.0)


def on_device(
    incoming_signals,
    receptor_linear_map,
    lock_linear_map,
    worth_linear_map,
    outbound_linear_map,
    selfward_extra,
    cluster_amplify_level,
    dwindle_powers,
    bisect_indicators,
    tutor_aggregated,
):
    length = incoming_signals.shape[0]
    lanes = LANES_EACH_HEAD
    blocks = lax.axis_size("ctx")
    mine = lax.axis_index("ctx")
    x_at, core_at = lax.axis_index("x"), lax.axis_index("core")
    tiles = GRID["x"] * GRID["core"]
    rows = GRID["y"]
    part = length // tiles
    all_frames = length * blocks

    w_mine, w_other = gather_rows(outbound_linear_map)

    receptor_linear_coeffs = jnp.dot(
        incoming_signals, receptor_linear_map, preferred_element_type=jnp.float32
    )[None]
    keys_raw = jnp.dot(incoming_signals, lock_linear_map, preferred_element_type=jnp.float32)[None]
    worth_linear_coeffs = jnp.dot(
        incoming_signals, worth_linear_map, preferred_element_type=jnp.float32
    )[None]
    lock_linear_coeffs, scale = key_norm(keys_raw)
    rate = -rate_span * (dwindle_powers.astype(jnp.float32) + 1.0) / float(CODES * all_frames)
    log_steps = rate.reshape(1, 1, lanes) + (
        bisect_indicators.astype(jnp.float32) * log_half
    ).reshape(1, length, 1)
    prefix_logarithm = jnp.cumsum(log_steps, axis=1)
    stacked_selfward_extras = selfward_extra.reshape(1, 1, lanes)
    gain_heads = cluster_amplify_level.reshape(1, 1, lanes)
    collated_additions = piece_summands(
        receptor_linear_coeffs, lock_linear_coeffs, prefix_logarithm
    )
    within_piece_share = jnp.einsum(
        "atn,ato->ano",
        lock_linear_coeffs * collated_additions[4],
        worth_linear_coeffs,
        precision=numeric_fidelity,
    )[0]
    last = prefix_logarithm[0, length - 1, :]
    half = lanes // 2
    packed = jnp.concatenate(
        [
            jnp.concatenate([within_piece_share[:half], within_piece_share[half:]], axis=1),
            jnp.broadcast_to(jnp.concatenate([last, last])[None], (8, 2 * lanes)),
        ],
        axis=0,
    )
    everyone = to_all(packed, "ctx", blocks)
    shares = jnp.concatenate([everyone[:, :half, :lanes], everyone[:, :half, lanes:]], axis=1)
    log_totals = everyone[:, half, :lanes]
    beginning_hidden_carryover = jnp.sum(
        weights_between(log_totals, mine, False)[:, :, None] * shares, axis=0
    )[None]
    generated_elements = slice_yields(
        receptor_linear_coeffs,
        lock_linear_coeffs,
        worth_linear_coeffs,
        stacked_selfward_extras,
        collated_additions,
        beginning_hidden_carryover,
    )
    unit, inverse = head_norm(generated_elements)
    normed = (unit * gain_heads).astype(jnp.bfloat16)

    sent = jnp.concatenate(
        [
            normed.reshape(tiles, part, lanes),
            tutor_aggregated.reshape(tiles, part, lanes),
        ],
        axis=2,
    )
    got = exchange(sent, TILE)
    order_x = (x_at - jnp.arange(GRID["x"])) % GRID["x"]
    order = jnp.concatenate([order_x * 2 + core_at, order_x * 2 + 1 - core_at])
    ordered = jnp.take(got[:, :, :lanes], order, axis=0).transpose(1, 0, 2).reshape(part, tiles * lanes)
    cut = tiles * lanes // 2
    partial_mixed = jnp.dot(
        ordered[:, :cut], w_mine, preferred_element_type=jnp.float32
    ) + jnp.dot(ordered[:, cut:], w_other, preferred_element_type=jnp.float32)
    pieces = partial_mixed.reshape(part, rows, tiles * lanes).transpose(1, 0, 2).astype(jnp.bfloat16)
    mixed = jnp.sum(exchange(pieces, "y").astype(jnp.float32), axis=0).astype(jnp.bfloat16)
    tutor = got[:, :, lanes:].transpose(1, 0, 2).reshape(part, tiles * lanes)
    diff = (mixed.astype(jnp.float32) - tutor.astype(jnp.float32)).astype(jnp.bfloat16)
    diff_all = to_all(diff, "y", rows).transpose(1, 0, 2).reshape(part, rows * tiles * lanes)
    over_columns = (((1,), (1,)), ((), ()))
    grads = jnp.concatenate(
        [
            lax.dot_general(diff_all, w_mine, over_columns, preferred_element_type=jnp.float32),
            lax.dot_general(diff_all, w_other, over_columns, preferred_element_type=jnp.float32),
        ],
        axis=1,
    )
    source = jnp.arange(tiles)
    place = (x_at - source // 2) % GRID["x"] + jnp.where(source % 2 == core_at, 0, GRID["x"])
    grads = jnp.take(grads.reshape(part, tiles, lanes).transpose(1, 0, 2), place, axis=0)
    back = exchange(
        jnp.concatenate(
            [
                grads.astype(jnp.bfloat16),
                mixed.reshape(part, tiles, lanes).transpose(1, 0, 2),
            ],
            axis=2,
        ),
        TILE,
    ).reshape(length, 2 * lanes)
    mixed_out = back[:, lanes:]
    grad_normed = back[:, :lanes].astype(jnp.float32)[None]

    outcome_sensitivity = head_norm_back(unit, inverse, gain_heads, grad_normed)
    reverse_sweeping = jnp.einsum(
        "atn,ato->ano", collated_additions[2], outcome_sensitivity, precision=numeric_fidelity
    )[0]
    later = to_all(
        jnp.concatenate([reverse_sweeping[:half], reverse_sweeping[half:]], axis=1), "ctx", blocks
    )
    later = jnp.concatenate([later[:, :, :lanes], later[:, :, lanes:]], axis=1)
    walking_hidden_carryover = jnp.sum(
        weights_between(log_totals, mine, True)[:, :, None] * later, axis=0
    )[None]
    receptor_sensitivity, sensitivity_whitened_guess, value_gradients = slice_sensitivities(
        receptor_linear_coeffs,
        lock_linear_coeffs,
        worth_linear_coeffs,
        stacked_selfward_extras,
        collated_additions,
        beginning_hidden_carryover,
        walking_hidden_carryover,
        outcome_sensitivity,
    )
    grad_keys = key_norm_back(keys_raw, scale, sensitivity_whitened_guess)
    return (
        mixed_out,
        receptor_sensitivity[0].astype(jnp.bfloat16),
        grad_keys[0].astype(jnp.bfloat16),
        value_gradients[0].astype(jnp.bfloat16),
    )


def solution(mesh):
    blocks = mesh.shape["ctx"]
    grid = Mesh(mesh.devices.reshape((blocks,) + tuple(GRID.values())), ("ctx",) + tuple(GRID))
    head = tuple(GRID)
    in_specs = (
        P("ctx", None),
        P(None, head),
        P(None, head),
        P(None, head),
        P(head, None),
        P(head),
        P(head),
        P(head),
        P("ctx"),
        P("ctx", head),
    )
    out_specs = (P("ctx", head), P("ctx", head), P("ctx", head), P("ctx", head))
    return jax.shard_map(
        on_device, mesh=grid, in_specs=in_specs, out_specs=out_specs, check_vma=False
    )
```

```python
import functools

import jax
import jax.numpy as jnp
from jax import lax
from jax.experimental import pallas as pl
from jax.experimental.pallas import tpu as pltpu
from jax.sharding import Mesh, PartitionSpec as P

LANES = 64
CODES = 64
GRID = {"y": 8, "x": 4, "core": 2}
STEPS = 8
COUNT_BASE = 64

epsilon = 1e-05
log_half = -0.6931471805599453
rate_span = 1.2
f32 = jnp.float32
bf16 = jnp.bfloat16


def nn(a, b):
    return lax.dot_general(
        a, b, (((1,), (0,)), ((), ())), precision=lax.Precision.HIGHEST, preferred_element_type=f32
    )


def nt(a, b):
    return lax.dot_general(
        a, b, (((1,), (1,)), ((), ())), precision=lax.Precision.HIGHEST, preferred_element_type=f32
    )


def tn(a, b):
    return nn(a.T, b)


def column(row):
    n = row.shape[1]
    at = lax.broadcasted_iota(jnp.int32, (n, n), 0)
    on = at == lax.broadcasted_iota(jnp.int32, (n, n), 1)
    return jnp.sum(jnp.where(on, row, 0.0), axis=1, keepdims=True)


def rates(codes_row, all_frames):
    return -rate_span * (column(codes_row.astype(f32)) + 1.0) / float(CODES * all_frames)


def over_channels(array):
    return jnp.mean(array, axis=0, keepdims=True)


def key_norm(keys_raw):
    scale = lax.rsqrt(over_channels(keys_raw * keys_raw) + epsilon)
    return keys_raw * scale * 0.125, scale


def fold(square):
    half = square.shape[0] // 2
    return jnp.concatenate([square[:half], square[half:]], axis=1)


def unfold(packed):
    return jnp.concatenate([packed[:, :LANES], packed[:, LANES:]], axis=0)


def causal(length):
    s = lax.broadcasted_iota(jnp.int32, (length, length), 0)
    return s <= lax.broadcasted_iota(jnp.int32, (length, length), 1)


def keys_kernel(all_frames, x, wk, wv, codes, halvings, payload, keys_raw, values, logs, acc):
    step = pl.program_id(0)

    @pl.when(step == 0)
    def _():
        acc[...] = jnp.zeros_like(acc)

    acc[...] += lax.dot_general(
        jnp.concatenate([wk[...], wv[...]], axis=0),
        x[...],
        (((1,), (1,)), ((), ())),
        preferred_element_type=f32,
    )

    @pl.when(step == STEPS - 1)
    def _():
        length = x.shape[0]
        raw, val = acc[:LANES], acc[LANES:]
        keys_raw[...] = raw
        values[...] = val
        keys, _ = key_norm(raw)
        rate = rates(codes[...], all_frames)
        marks = jnp.broadcast_to(halvings[...].astype(f32).astype(bf16), (16, length))
        ones = jnp.where(causal(length), 1.0, 0.0).astype(bf16)
        counted = jnp.dot(marks, ones, preferred_element_type=f32)[:1]
        at = (lax.broadcasted_iota(jnp.int32, (1, length), 1) + 1).astype(f32)
        prefix = rate * at + log_half * counted
        logs[...] = prefix
        total = counted[:, length - 1 :]
        closing = jnp.exp(rate * float(length) + log_half * total - prefix)
        share = fold(nt(keys * closing, val)).astype(bf16)
        high = jnp.floor(total * (1.0 / COUNT_BASE))
        low = total - high * COUNT_BASE
        top = lax.broadcasted_iota(jnp.int32, (16, 2 * LANES), 0) == 0
        counts = jnp.where(top, high, low).astype(bf16)
        half = LANES // 2
        for z in range(payload.shape[0]):
            payload[z, :half] = share
            payload[z, half:] = counts


def reads_kernel(
    x, wr, keys_raw, values, logs, extra, tutor, reads, scores, local, t0, t1, t2, t3, acc, held
):
    step = pl.program_id(0)

    @pl.when(step == 0)
    def _():
        acc[...] = jnp.zeros_like(acc)

    acc[...] += lax.dot_general(
        wr[...], x[...], (((1,), (1,)), ((), ())), preferred_element_type=f32
    )

    @pl.when(step == STEPS - 1)
    def _():
        length = x.shape[0]
        recept = acc[...]
        reads[...] = recept
        keys, _ = key_norm(keys_raw[...])
        prefix = logs[...]
        val = values[...]
        masked = jnp.where(
            causal(length), tn(keys * jnp.exp(-prefix), recept * jnp.exp(prefix)), 0.0
        )
        scores[...] = masked
        own = jnp.sum(recept * column(extra[...]) * keys, axis=0, keepdims=True)
        local[...] = nn(val, masked) + own * val
        by_frame = tutor[...].astype(f32).T.astype(bf16)
        tiles = GRID["x"] * GRID["core"]
        part = length // tiles
        for i in range(tiles):
            held[i] = fold(by_frame[i * part : (i + 1) * part])
        at = lax.axis_index("x")
        for s, out in enumerate((t0, t1, t2, t3)):
            to = lax.rem(at + s, GRID["x"])
            for c in range(2):
                out[c] = held[to * 2 + c]


def decays(everyone, rate, z, length):
    half = LANES // 2
    total = everyone[z, half : half + 1].astype(f32) * COUNT_BASE + everyone[
        z, half + 1 : half + 2
    ].astype(f32)
    return jnp.exp(rate * float(length) + log_half * total)


def folded_rates(codes_row, all_frames):
    return fold(jnp.broadcast_to(rates(codes_row, all_frames), (LANES, LANES)))


def yields_kernel(all_frames, everyone, local, reads, logs, codes, gain, sent, start, unit, inverse):
    length = local.shape[1]
    mine = lax.axis_index("ctx")
    half = LANES // 2
    rate = folded_rates(codes[...], all_frames)
    state = jnp.zeros((half, 2 * LANES), f32)
    for z in range(everyone.shape[0] - 1):
        longer = decays(everyone, rate, z, length) * state + everyone[z, :half].astype(f32)
        state = jnp.where(z < mine, longer, state)
    begin = unfold(state)
    start[...] = begin
    y = local[...] + tn(begin, reads[...] * jnp.exp(logs[...]))
    centred = y - over_channels(y)
    inv = lax.rsqrt(over_channels(centred * centred) + epsilon)
    inverse[...] = inv
    unit[...] = centred * inv
    normed = (centred * inv * column(gain[...])).T.astype(bf16)
    tiles = GRID["x"] * GRID["core"]
    part = length // tiles
    for i in range(tiles):
        block = fold(normed[i * part : (i + 1) * part])
        for j in range(GRID["y"]):
            sent[j * tiles + i] = block


def spread(blocks):
    cols = []
    for a, b in zip(blocks[::2], blocks[1::2]):
        cols.append(
            jnp.concatenate(
                [
                    jnp.concatenate([a[:, :LANES], b[:, :LANES]], axis=1),
                    jnp.concatenate([a[:, LANES:], b[:, LANES:]], axis=1),
                ],
                axis=0,
            )
        )
    return jnp.concatenate(cols, axis=1)


def by_source(mine, other, x, c):
    step = lax.rem(lax.axis_index("x") - x + GRID["x"], GRID["x"])
    core = lax.axis_index("core")
    return jnp.where(core == c, mine[step, core], other[step, core])


def middle_kernel(
    got, t_mine, t_other, w0, w1, w2, w3, v0, v1, v2, v3, sent, m0, m1, m2, m3, held
):
    at, core = lax.axis_index("x"), lax.axis_index("core")
    tiles = GRID["x"] * GRID["core"]
    rows = GRID["y"]
    group = min(4, rows)
    chunks = []
    for ws, c in (((w0, w1, w2, w3), core), ((v0, v1, v2, v3), 1 - core)):
        for s, w in enumerate(ws):
            x = lax.rem(at - s + GRID["x"], GRID["x"])
            for y in range(0, rows, group):
                chunks.append((w, y, [(y + g) * tiles + x * 2 + c for g in range(group)]))
    acc = None
    for w, y, places in chunks:
        weights = w[y : y + group].reshape(group * LANES, tiles * LANES)
        term = jnp.dot(spread([got[p] for p in places]), weights, preferred_element_type=f32)
        acc = term if acc is None else acc + term
    mixed = acc.astype(bf16)
    for i in range(tiles):
        held[i] = fold(mixed[:, i * LANES : (i + 1) * LANES])
    for s, out in enumerate((m0, m1, m2, m3)):
        to = lax.rem(at + s, GRID["x"])
        for c in range(2):
            out[c] = held[to * 2 + c]
    wanted = spread([by_source(t_mine, t_other, i // 2, i % 2) for i in range(tiles)])
    diff = (mixed.astype(f32) - wanted.astype(f32)).astype(bf16)
    for w, y, places in chunks:
        weights = w[y : y + group].reshape(group * LANES, tiles * LANES)
        grads = lax.dot_general(
            diff, weights, (((1,), (1,)), ((), ())), preferred_element_type=f32
        ).astype(bf16)
        for g, p in enumerate(places):
            sent[p] = fold(grads[:, g * LANES : (g + 1) * LANES])


def back_kernel(got, unit, inverse, gain, reads, logs, payload, sensitivity):
    tiles = GRID["x"] * GRID["core"]
    frames = []
    for i in range(tiles):
        total = got[i].astype(f32)
        for j in range(1, GRID["y"]):
            total = total + got[j * tiles + i].astype(f32)
        frames.append(unfold(total))
    scaled = jnp.concatenate(frames, axis=0).T * column(gain[...])
    each = unit[...]
    grad = inverse[...] * (
        scaled - over_channels(scaled) - each * over_channels(scaled * each)
    )
    sensitivity[...] = grad
    share = fold(nt(reads[...] * jnp.exp(logs[...]), grad)).astype(bf16)
    for z in range(payload.shape[0]):
        payload[z] = share


def window_kernel(
    m_mine, m_other, reads, keys_raw, values, logs, extra, scores, start, sensitivity,
    mixed_out, grad_reads, part_keys, part_values,
):
    length = reads.shape[1]
    tiles = GRID["x"] * GRID["core"]
    mixed_out[...] = (
        jnp.concatenate(
            [
                unfold(by_source(m_mine, m_other, i // 2, i % 2).astype(f32))
                for i in range(tiles)
            ],
            axis=0,
        ).T.astype(bf16)
    )
    recept, val, grad = reads[...], values[...], sensitivity[...]
    keys, _ = key_norm(keys_raw[...])
    prefix = logs[...]
    grow, shrink = jnp.exp(prefix), jnp.exp(-prefix)
    own_weight = column(extra[...])
    twofold = jnp.where(causal(length), tn(val, grad), 0.0)
    progressive = jnp.sum(grad * val, axis=0, keepdims=True) * own_weight
    own = jnp.sum(recept * own_weight * keys, axis=0, keepdims=True)
    grad_reads[...] = (
        grow * (nn(start[...], grad) + nn(keys * shrink, twofold)) + progressive * keys
    ).astype(bf16)
    part_keys[...] = shrink * nt(recept * grow, twofold) + progressive * recept
    part_values[...] = nt(grad, scores[...]) + own * grad


def final_kernel(
    all_frames, later, everyone, part_keys, part_values, keys_raw, values, logs, codes,
    grad_keys, grad_values,
):
    length = keys_raw.shape[1]
    mine = lax.axis_index("ctx")
    half = LANES // 2
    rate = folded_rates(codes[...], all_frames)
    state = jnp.zeros((half, 2 * LANES), f32)
    for z in range(everyone.shape[0] - 1, 0, -1):
        longer = decays(everyone, rate, z, length) * state + later[z].astype(f32)
        state = jnp.where(z > mine, longer, state)
    walking = unfold(state)
    raw = keys_raw[...]
    keys, scale = key_norm(raw)
    prefix = logs[...]
    closing = jnp.exp(prefix[:, length - 1 :] - prefix)
    grad = part_keys[...] + closing * nn(walking, values[...])
    grad_values[...] = (part_values[...] + tn(walking, keys * closing)).astype(bf16)
    grad_keys[...] = (
        0.125 * scale * (grad - scale * scale * raw * over_channels(raw * grad))
    ).astype(bf16)


def call(kernel, outs, args, cost=1 << 23, **more):
    return pl.pallas_call(
        kernel,
        cost_estimate=pl.CostEstimate(flops=1 << 30, transcendentals=0, bytes_accessed=cost),
        out_shape=[jax.ShapeDtypeStruct(shape, kind) for shape, kind in outs],
        **more,
    )(*args)


def exchange(array, axis):
    return lax.all_to_all(array, axis, 0, 0)


def along_x(parts):
    n = GRID["x"]
    return parts[:1] + [
        lax.ppermute(parts[s], "x", [(i, (i + s) % n) for i in range(n)]) for s in range(1, n)
    ]


def swap(array):
    return lax.ppermute(array, "core", [(0, 1), (1, 0)])


def on_device(
    incoming_signals,
    receptor_linear_map,
    lock_linear_map,
    worth_linear_map,
    outbound_linear_map,
    selfward_extra,
    cluster_amplify_level,
    dwindle_powers,
    bisect_indicators,
    tutor_aggregated,
):
    length, width = incoming_signals.shape
    blocks = lax.axis_size("ctx")
    tiles, rows = GRID["x"] * GRID["core"], GRID["y"]
    part = length // tiles
    all_frames = length * blocks
    half = LANES // 2
    head = tuple(GRID)
    flat = (LANES, length)
    block = (part // 2, 2 * LANES)
    barrier = lax.optimization_barrier

    columns = exchange(
        outbound_linear_map.reshape(LANES, rows, tiles * LANES).transpose(1, 0, 2), "y"
    )

    codes = dwindle_powers.reshape(1, LANES)
    extra = selfward_extra.reshape(1, LANES)
    gain = cluster_amplify_level.reshape(1, LANES)
    halvings = bisect_indicators.reshape(1, length)

    depth = width // STEPS
    whole = pl.BlockSpec(memory_space=pltpu.VMEM)
    by_step = [
        pl.BlockSpec((length, depth), lambda k: (0, k)),
        pl.BlockSpec((LANES, depth), lambda k: (0, k)),
    ]
    serial = pltpu.CompilerParams(dimension_semantics=("arbitrary",))
    payload, keys_raw, values, logs = call(
        functools.partial(keys_kernel, all_frames),
        [((blocks, half + 16, 2 * LANES), bf16), (flat, f32), (flat, f32), (flat, f32)],
        (incoming_signals, lock_linear_map.T, worth_linear_map.T, codes, halvings),
        grid=(STEPS,),
        in_specs=[by_step[0], by_step[1], by_step[1], whole, whole],
        out_specs=[whole] * 4,
        scratch_shapes=[pltpu.VMEM((2 * LANES, length), f32)],
        compiler_params=serial,
    )
    reads, scores, local, *tutor = call(
        reads_kernel,
        [(flat, f32), ((length, length), f32), (flat, f32)] + [((2,) + block, bf16)] * GRID["x"],
        (
            incoming_signals, receptor_linear_map.T, keys_raw, values, logs, extra,
            tutor_aggregated.T,
        ),
        grid=(STEPS,),
        in_specs=[by_step[0], by_step[1]] + [whole] * 5,
        out_specs=[whole] * (3 + GRID["x"]),
        scratch_shapes=[pltpu.VMEM(flat, f32), pltpu.VMEM((tiles,) + block, bf16)],
        compiler_params=serial,
    )
    payload, columns, local, *tutor = barrier((payload, columns, local, *tutor))
    everyone = exchange(payload, "ctx")
    w_mine = along_x([columns] * GRID["x"])
    sent, start, unit, inverse = call(
        functools.partial(yields_kernel, all_frames),
        [((rows * tiles,) + block, bf16), ((LANES, LANES), f32), (flat, f32), ((1, length), f32)],
        (everyone, local, reads, logs, codes, gain),
    )
    got = exchange(sent, head)
    w_other = [swap(w) for w in w_mine]
    tutor = jnp.stack(along_x(tutor))
    sent, *mixed = call(
        middle_kernel,
        [((rows * tiles,) + block, bf16)] + [((2,) + block, bf16)] * GRID["x"],
        (got, tutor, swap(tutor), *w_mine, *w_other),
        scratch_shapes=[pltpu.VMEM((tiles,) + block, bf16)],
    )
    got = exchange(sent, head)
    mixed = jnp.stack(along_x(mixed))
    payload, sensitivity = call(
        back_kernel,
        [((blocks, half, 2 * LANES), bf16), (flat, f32)],
        (got, unit, inverse, gain, reads, logs),
    )
    later = exchange(payload, "ctx")
    mixed_out, grad_reads, part_keys, part_values = call(
        window_kernel,
        [(flat, bf16), (flat, bf16), (flat, f32), (flat, f32)],
        (mixed, swap(mixed), reads, keys_raw, values, logs, extra, scores, start, sensitivity),
    )
    grad_keys, grad_values = call(
        functools.partial(final_kernel, all_frames),
        [(flat, bf16), (flat, bf16)],
        (later, everyone, part_keys, part_values, keys_raw, values, logs, codes),
    )
    return (mixed_out.T, grad_reads.T, grad_keys.T, grad_values.T)


def solution(mesh):
    blocks = mesh.shape["ctx"]
    grid = Mesh(mesh.devices.reshape((blocks,) + tuple(GRID.values())), ("ctx",) + tuple(GRID))
    head = tuple(GRID)
    in_specs = (
        P("ctx", None),
        P(None, head),
        P(None, head),
        P(None, head),
        P(head, None),
        P(head),
        P(head),
        P(head),
        P("ctx"),
        P("ctx", head),
    )
    out_specs = (P("ctx", head), P("ctx", head), P("ctx", head), P("ctx", head))
    return jax.shard_map(
        on_device, mesh=grid, in_specs=in_specs, out_specs=out_specs, check_vma=False
    )
```

```python
import functools

import jax
import jax.numpy as jnp
from jax import lax
from jax.experimental import pallas as pl
from jax.experimental.pallas import tpu as pltpu
from jax.sharding import Mesh, PartitionSpec as P

LANES = 64
CODES = 64
GRID = {"y": 8, "x": 4, "core": 2}
STEPS = 8
COUNT_BASE = 64

epsilon = 1e-05
log_half = -0.6931471805599453
rate_span = 1.2
f32 = jnp.float32
bf16 = jnp.bfloat16


def nn(a, b):
    return lax.dot_general(
        a, b, (((1,), (0,)), ((), ())), precision=lax.Precision.HIGHEST, preferred_element_type=f32
    )


def nt(a, b):
    return lax.dot_general(
        a, b, (((1,), (1,)), ((), ())), precision=lax.Precision.HIGHEST, preferred_element_type=f32
    )


def tn(a, b):
    return nn(a.T, b)


def once(a, b, dims):
    return lax.dot_general(
        a.astype(bf16), b.astype(bf16), (dims, ((), ())), preferred_element_type=f32
    )


def column(row):
    n = row.shape[1]
    at = lax.broadcasted_iota(jnp.int32, (n, n), 0)
    on = at == lax.broadcasted_iota(jnp.int32, (n, n), 1)
    return jnp.sum(jnp.where(on, row, 0.0), axis=1, keepdims=True)


def rates(codes_row, all_frames):
    return -rate_span * (column(codes_row.astype(f32)) + 1.0) / float(CODES * all_frames)


def over_channels(array):
    return jnp.mean(array, axis=0, keepdims=True)


def key_norm(keys_raw):
    scale = lax.rsqrt(over_channels(keys_raw * keys_raw) + epsilon)
    return keys_raw * scale * 0.125, scale


def fold(square):
    half = square.shape[0] // 2
    return jnp.concatenate([square[:half], square[half:]], axis=1)


def unfold(packed):
    return jnp.concatenate([packed[:, :LANES], packed[:, LANES:]], axis=0)


def causal(length):
    s = lax.broadcasted_iota(jnp.int32, (length, length), 0)
    return s <= lax.broadcasted_iota(jnp.int32, (length, length), 1)


def project_kernel(
    all_frames, x, wr, wk, wv, codes, halvings, extra, tutor,
    payload, reads, keys_raw, values, logs, scores, local, t0, t1, t2, t3, acc, held,
):
    step = pl.program_id(0)

    @pl.when(step == 0)
    def _():
        acc[...] = jnp.zeros_like(acc)

    acc[...] += lax.dot_general(
        x[...],
        jnp.concatenate([wr[...], wk[...], wv[...]], axis=0),
        (((1,), (1,)), ((), ())),
        preferred_element_type=f32,
    )

    @pl.when(step == STEPS - 1)
    def _():
        length = x.shape[0]
        whole = acc[...].T
        recept, raw, val = whole[:LANES], whole[LANES : 2 * LANES], whole[2 * LANES :]
        reads[...] = recept
        keys_raw[...] = raw
        values[...] = val
        keys, _ = key_norm(raw)
        rate = rates(codes[...], all_frames)
        marks = jnp.broadcast_to(halvings[...].astype(f32).astype(bf16), (16, length))
        mask = causal(length)
        ones = jnp.where(mask, 1.0, 0.0).astype(bf16)
        counted = jnp.dot(marks, ones, preferred_element_type=f32)[:1]
        at = (lax.broadcasted_iota(jnp.int32, (1, length), 1) + 1).astype(f32)
        prefix = rate * at + log_half * counted
        logs[...] = prefix
        total = counted[:, length - 1 :]
        closing = jnp.exp(rate * float(length) + log_half * total - prefix)
        share = fold(nt(keys * closing, val)).astype(bf16)
        high = jnp.floor(total * (1.0 / COUNT_BASE))
        low = total - high * COUNT_BASE
        top = lax.broadcasted_iota(jnp.int32, (16, 2 * LANES), 0) == 0
        counts = jnp.where(top, high, low).astype(bf16)
        half = LANES // 2
        for z in range(payload.shape[0]):
            payload[z, :half] = share
            payload[z, half:] = counts
        masked = jnp.where(mask, tn(keys * jnp.exp(-prefix), recept * jnp.exp(prefix)), 0.0)
        scores[...] = masked.astype(bf16)
        own = jnp.sum(recept * column(extra[...]) * keys, axis=0, keepdims=True)
        local[...] = nn(val, masked) + own * val
        by_frame = tutor[...].astype(f32).T.astype(bf16)
        tiles = GRID["x"] * GRID["core"]
        part = length // tiles
        for i in range(tiles):
            held[i] = fold(by_frame[i * part : (i + 1) * part])
        place = lax.axis_index("x")
        for s, out in enumerate((t0, t1, t2, t3)):
            to = lax.rem(place + s, GRID["x"])
            for c in range(2):
                out[c] = held[to * 2 + c]


def decays(everyone, rate, z, length):
    half = LANES // 2
    total = everyone[z, half : half + 1].astype(f32) * COUNT_BASE + everyone[
        z, half + 1 : half + 2
    ].astype(f32)
    return jnp.exp(rate * float(length) + log_half * total)


def folded_rates(codes_row, all_frames):
    return fold(jnp.broadcast_to(rates(codes_row, all_frames), (LANES, LANES)))


def yields_kernel(all_frames, everyone, local, reads, logs, codes, gain, sent, start, unit, inverse):
    length = local.shape[1]
    mine = lax.axis_index("ctx")
    half = LANES // 2
    rate = folded_rates(codes[...], all_frames)
    state = jnp.zeros((half, 2 * LANES), f32)
    for z in range(everyone.shape[0] - 1):
        longer = decays(everyone, rate, z, length) * state + everyone[z, :half].astype(f32)
        state = jnp.where(z < mine, longer, state)
    begin = unfold(state)
    start[...] = begin
    y = local[...] + tn(begin, reads[...] * jnp.exp(logs[...]))
    centred = y - over_channels(y)
    inv = lax.rsqrt(over_channels(centred * centred) + epsilon)
    inverse[...] = inv
    unit[...] = centred * inv
    normed = (centred * inv * column(gain[...])).T.astype(bf16)
    tiles = GRID["x"] * GRID["core"]
    part = length // tiles
    for i in range(tiles):
        block = fold(normed[i * part : (i + 1) * part])
        for j in range(GRID["y"]):
            sent[j * tiles + i] = block


def spread(blocks):
    cols = []
    for a, b in zip(blocks[::2], blocks[1::2]):
        cols.append(
            jnp.concatenate(
                [
                    jnp.concatenate([a[:, :LANES], b[:, :LANES]], axis=1),
                    jnp.concatenate([a[:, LANES:], b[:, LANES:]], axis=1),
                ],
                axis=0,
            )
        )
    return jnp.concatenate(cols, axis=1)


def by_source(mine, other, x, c):
    step = lax.rem(lax.axis_index("x") - x + GRID["x"], GRID["x"])
    core = lax.axis_index("core")
    return jnp.where(core == c, mine[step, core], other[step, core])


def middle_kernel(
    got, t_mine, t_other, w0, w1, w2, w3, v0, v1, v2, v3, sent, m0, m1, m2, m3, held, weights, sems
):
    copies = []
    for n, source in enumerate((w0, v0, w1, v1, w2, v2, w3, v3)):
        copies.append(pltpu.make_async_copy(source, weights.at[n], sems.at[n]))
        copies[n].start()
    at, core = lax.axis_index("x"), lax.axis_index("core")
    tiles = GRID["x"] * GRID["core"]
    rows = GRID["y"]
    group = min(4, rows)
    chunks = []
    for s in range(GRID["x"]):
        x = lax.rem(at - s + GRID["x"], GRID["x"])
        for n, c in ((2 * s, core), (2 * s + 1, 1 - core)):
            for y in range(0, rows, group):
                chunks.append((n, y, [(y + g) * tiles + x * 2 + c for g in range(group)]))
    acc = None
    for n, y, places in chunks:
        if y == 0:
            copies[n].wait()
        part = weights[n, y : y + group].reshape(group * LANES, tiles * LANES)
        term = jnp.dot(spread([got[p] for p in places]), part, preferred_element_type=f32)
        acc = term if acc is None else acc + term
    mixed = acc.astype(bf16)
    for i in range(tiles):
        held[i] = fold(mixed[:, i * LANES : (i + 1) * LANES])
    for s, out in enumerate((m0, m1, m2, m3)):
        to = lax.rem(at + s, GRID["x"])
        for c in range(2):
            out[c] = held[to * 2 + c]
    wanted = spread([by_source(t_mine, t_other, i // 2, i % 2) for i in range(tiles)])
    diff = (mixed.astype(f32) - wanted.astype(f32)).astype(bf16)
    for n, y, places in chunks:
        part = weights[n, y : y + group].reshape(group * LANES, tiles * LANES)
        grads = lax.dot_general(
            diff, part, (((1,), (1,)), ((), ())), preferred_element_type=f32
        ).astype(bf16)
        for g, p in enumerate(places):
            sent[p] = fold(grads[:, g * LANES : (g + 1) * LANES])


def back_kernel(got, unit, inverse, gain, reads, logs, payload, sensitivity):
    tiles = GRID["x"] * GRID["core"]
    frames = []
    for i in range(tiles):
        total = got[i].astype(f32)
        for j in range(1, GRID["y"]):
            total = total + got[j * tiles + i].astype(f32)
        frames.append(unfold(total))
    scaled = jnp.concatenate(frames, axis=0).T * column(gain[...])
    each = unit[...]
    grad = inverse[...] * (
        scaled - over_channels(scaled) - each * over_channels(scaled * each)
    )
    sensitivity[...] = grad
    share = fold(nt(reads[...] * jnp.exp(logs[...]), grad)).astype(bf16)
    for z in range(payload.shape[0]):
        payload[z] = share


def window_kernel(
    m_mine, m_other, reads, keys_raw, values, logs, extra, scores, start, sensitivity,
    mixed_out, grad_reads, part_keys, part_values,
):
    length = reads.shape[1]
    tiles = GRID["x"] * GRID["core"]
    mixed_out[...] = (
        jnp.concatenate(
            [
                unfold(by_source(m_mine, m_other, i // 2, i % 2).astype(f32))
                for i in range(tiles)
            ],
            axis=0,
        ).T.astype(bf16)
    )
    recept, val, grad = reads[...], values[...], sensitivity[...]
    keys, _ = key_norm(keys_raw[...])
    prefix = logs[...]
    grow, shrink = jnp.exp(prefix), jnp.exp(-prefix)
    own_weight = column(extra[...])
    twofold = jnp.where(causal(length), once(val.T, grad, ((1,), (0,))), 0.0).astype(bf16)
    progressive = jnp.sum(grad * val, axis=0, keepdims=True) * own_weight
    own = jnp.sum(recept * own_weight * keys, axis=0, keepdims=True)
    grad_reads[...] = (
        grow * (nn(start[...], grad) + once(keys * shrink, twofold, ((1,), (0,)))) + progressive * keys
    ).astype(bf16)
    part_keys[...] = shrink * once(recept * grow, twofold, ((1,), (1,))) + progressive * recept
    part_values[...] = once(grad, scores[...], ((1,), (1,))) + own * grad


def final_kernel(
    all_frames, later, everyone, part_keys, part_values, keys_raw, values, logs, codes,
    grad_keys, grad_values,
):
    length = keys_raw.shape[1]
    mine = lax.axis_index("ctx")
    half = LANES // 2
    rate = folded_rates(codes[...], all_frames)
    state = jnp.zeros((half, 2 * LANES), f32)
    for z in range(everyone.shape[0] - 1, 0, -1):
        longer = decays(everyone, rate, z, length) * state + later[z].astype(f32)
        state = jnp.where(z > mine, longer, state)
    walking = unfold(state)
    raw = keys_raw[...]
    keys, scale = key_norm(raw)
    prefix = logs[...]
    closing = jnp.exp(prefix[:, length - 1 :] - prefix)
    grad = part_keys[...] + closing * nn(walking, values[...])
    grad_values[...] = (part_values[...] + tn(walking, keys * closing)).astype(bf16)
    grad_keys[...] = (
        0.125 * scale * (grad - scale * scale * raw * over_channels(raw * grad))
    ).astype(bf16)


def call(kernel, outs, args, cost=1 << 23, **more):
    return pl.pallas_call(
        kernel,
        cost_estimate=pl.CostEstimate(flops=1 << 30, transcendentals=0, bytes_accessed=cost),
        out_shape=[jax.ShapeDtypeStruct(shape, kind) for shape, kind in outs],
        **more,
    )(*args)


def exchange(array, axis):
    return lax.all_to_all(array, axis, 0, 0)


def along_x(parts):
    n = GRID["x"]
    return parts[:1] + [
        lax.ppermute(parts[s], "x", [(i, (i + s) % n) for i in range(n)]) for s in range(1, n)
    ]


def swap(array):
    return lax.ppermute(array, "core", [(0, 1), (1, 0)])


def on_device(
    incoming_signals,
    receptor_linear_map,
    lock_linear_map,
    worth_linear_map,
    outbound_linear_map,
    selfward_extra,
    cluster_amplify_level,
    dwindle_powers,
    bisect_indicators,
    tutor_aggregated,
):
    length, width = incoming_signals.shape
    blocks = lax.axis_size("ctx")
    tiles, rows = GRID["x"] * GRID["core"], GRID["y"]
    part = length // tiles
    all_frames = length * blocks
    half = LANES // 2
    head = tuple(GRID)
    flat = (LANES, length)
    block = (part // 2, 2 * LANES)
    barrier = lax.optimization_barrier

    columns = exchange(
        outbound_linear_map.reshape(LANES, rows, tiles * LANES).transpose(1, 0, 2), "y"
    )

    codes = dwindle_powers.reshape(1, LANES)
    extra = selfward_extra.reshape(1, LANES)
    gain = cluster_amplify_level.reshape(1, LANES)
    halvings = bisect_indicators.reshape(1, length)

    depth = width // STEPS
    whole = pl.BlockSpec(memory_space=pltpu.VMEM)
    by_step = [
        pl.BlockSpec((length, depth), lambda k: (0, k)),
        pl.BlockSpec((LANES, depth), lambda k: (0, k)),
    ]
    serial = pltpu.CompilerParams(dimension_semantics=("arbitrary",))
    payload, reads, keys_raw, values, logs, scores, local, *tutor = call(
        functools.partial(project_kernel, all_frames),
        [
            ((blocks, half + 16, 2 * LANES), bf16), (flat, f32), (flat, f32), (flat, f32),
            (flat, f32), ((length, length), bf16), (flat, f32),
        ]
        + [((2,) + block, bf16)] * GRID["x"],
        (
            incoming_signals, receptor_linear_map.T, lock_linear_map.T, worth_linear_map.T,
            codes, halvings, extra, tutor_aggregated.T,
        ),
        grid=(STEPS,),
        in_specs=[by_step[0]] + [by_step[1]] * 3 + [whole] * 4,
        out_specs=[whole] * (7 + GRID["x"]),
        scratch_shapes=[
            pltpu.VMEM((length, 3 * LANES), f32), pltpu.VMEM((tiles,) + block, bf16),
        ],
        compiler_params=serial,
    )
    tutor = jnp.stack(along_x(tutor))
    payload, columns, tutor = barrier((payload, columns, tutor))
    everyone = exchange(payload, "ctx")
    w_mine = along_x([columns] * GRID["x"])
    sent, start, unit, inverse = call(
        functools.partial(yields_kernel, all_frames),
        [((rows * tiles,) + block, bf16), ((LANES, LANES), f32), (flat, f32), ((1, length), f32)],
        (everyone, local, reads, logs, codes, gain),
    )
    got = exchange(sent, head)
    w_other = [swap(w) for w in w_mine]
    sent, *mixed = call(
        middle_kernel,
        [((rows * tiles,) + block, bf16)] + [((2,) + block, bf16)] * GRID["x"],
        (got, tutor, swap(tutor), *w_mine, *w_other),
        in_specs=[whole] * 3 + [pl.BlockSpec(memory_space=pl.ANY)] * (2 * GRID["x"]),
        scratch_shapes=[
            pltpu.VMEM((tiles,) + block, bf16),
            pltpu.VMEM((2 * GRID["x"], rows, LANES, tiles * LANES), bf16),
            pltpu.SemaphoreType.DMA((2 * GRID["x"],)),
        ],
    )
    got = exchange(sent, head)
    mixed = jnp.stack(along_x(mixed))
    payload, sensitivity = call(
        back_kernel,
        [((blocks, half, 2 * LANES), bf16), (flat, f32)],
        (got, unit, inverse, gain, reads, logs),
    )
    later = exchange(payload, "ctx")
    mixed_out, grad_reads, part_keys, part_values = call(
        window_kernel,
        [(flat, bf16), (flat, bf16), (flat, f32), (flat, f32)],
        (mixed, swap(mixed), reads, keys_raw, values, logs, extra, scores, start, sensitivity),
    )
    grad_keys, grad_values = call(
        functools.partial(final_kernel, all_frames),
        [(flat, bf16), (flat, bf16)],
        (later, everyone, part_keys, part_values, keys_raw, values, logs, codes),
    )
    return (mixed_out.T, grad_reads.T, grad_keys.T, grad_values.T)


def solution(mesh):
    blocks = mesh.shape["ctx"]
    grid = Mesh(mesh.devices.reshape((blocks,) + tuple(GRID.values())), ("ctx",) + tuple(GRID))
    head = tuple(GRID)
    in_specs = (
        P("ctx", None),
        P(None, head),
        P(None, head),
        P(None, head),
        P(head, None),
        P(head),
        P(head),
        P(head),
        P("ctx"),
        P("ctx", head),
    )
    out_specs = (P("ctx", head), P("ctx", head), P("ctx", head), P("ctx", head))
    return jax.shard_map(
        on_device, mesh=grid, in_specs=in_specs, out_specs=out_specs, check_vma=False
    )
```

```python
import functools

import jax
import jax.numpy as jnp
from jax import lax
from jax.experimental import pallas as pl
from jax.experimental.pallas import tpu as pltpu
from jax.sharding import Mesh, PartitionSpec as P

LANES = 64
CODES = 64
GRID = {"y": 8, "x": 4, "core": 2}
STEPS = 4
COUNT_BASE = 64

epsilon = 1e-05
log_half = -0.6931471805599453
rate_span = 1.2
f32 = jnp.float32
bf16 = jnp.bfloat16


def once(a, b, dims):
    return lax.dot_general(
        a.astype(bf16), b.astype(bf16), (dims, ((), ())), preferred_element_type=f32
    )


def split(a):
    high = a.astype(bf16)
    return high, (a - high.astype(f32)).astype(bf16)


def thrice(a, b):
    (a_high, a_low), (b_high, b_low) = split(a), split(b)
    if a.shape[1] <= LANES:
        return once(
            jnp.concatenate([a_high, a_high, a_low], axis=1),
            jnp.concatenate([b_high, b_low, b_high], axis=0),
            ((1,), (0,)),
        )
    both = once(jnp.concatenate([a_high, a_low], axis=0), b_high, ((1,), (0,)))
    rows = a.shape[0]
    return both[:rows] + both[rows:] + once(a_high, b_low, ((1,), (0,)))


def column(row):
    n = row.shape[1]
    at = lax.broadcasted_iota(jnp.int32, (n, n), 0)
    on = at == lax.broadcasted_iota(jnp.int32, (n, n), 1)
    return jnp.sum(jnp.where(on, row, 0.0), axis=1, keepdims=True)


def rates(codes_row, all_frames):
    return -rate_span * (column(codes_row.astype(f32)) + 1.0) / float(CODES * all_frames)


def over_channels(array):
    return jnp.mean(array, axis=0, keepdims=True)


def key_norm(keys_raw):
    scale = lax.rsqrt(over_channels(keys_raw * keys_raw) + epsilon)
    return keys_raw * scale * 0.125, scale


def fold(square):
    half = square.shape[0] // 2
    return jnp.concatenate([square[:half], square[half:]], axis=1)


def unfold(packed):
    return jnp.concatenate([packed[:, :LANES], packed[:, LANES:]], axis=0)


def earlier(length):
    s = lax.broadcasted_iota(jnp.int32, (length, length), 0)
    return s < lax.broadcasted_iota(jnp.int32, (length, length), 1)


def project_kernel(
    all_frames, x, wr, wk, wv, codes, halvings, extra, tutor,
    payload, reads, keys_raw, values, logs, scores, local, t0, t1, t2, t3, acc, held,
):
    step = pl.program_id(0)

    @pl.when(step == 0)
    def _():
        acc[...] = jnp.zeros_like(acc)

    acc[...] += lax.dot_general(
        x[...],
        jnp.concatenate([wr[...], wk[...], wv[...]], axis=0),
        (((1,), (1,)), ((), ())),
        preferred_element_type=f32,
    )

    @pl.when(step == STEPS - 1)
    def _():
        length = x.shape[0]
        whole = acc[...].T
        recept, raw, val = whole[:LANES], whole[LANES : 2 * LANES], whole[2 * LANES :]
        reads[...] = recept
        keys_raw[...] = raw
        values[...] = val
        keys, _ = key_norm(raw)
        rate = rates(codes[...], all_frames)
        marks = jnp.broadcast_to(halvings[...].astype(f32).astype(bf16), (16, length))
        mask = earlier(length)
        ones = jnp.where(mask, 1.0, 0.0).astype(bf16)
        counted = (jnp.dot(marks, ones, preferred_element_type=f32) + marks.astype(f32))[:1]
        at = (lax.broadcasted_iota(jnp.int32, (1, length), 1) + 1).astype(f32)
        prefix = rate * at + log_half * counted
        logs[...] = prefix
        total = counted[:, length - 1 :]
        closing = jnp.exp(rate * float(length) + log_half * total - prefix)
        share = fold(once(keys * closing, val, ((1,), (1,)))).astype(bf16)
        high = jnp.floor(total * (1.0 / COUNT_BASE))
        low = total - high * COUNT_BASE
        top = lax.broadcasted_iota(jnp.int32, (16, 2 * LANES), 0) == 0
        counts = jnp.where(top, high, low).astype(bf16)
        half = LANES // 2
        for z in range(payload.shape[0]):
            payload[z, :half] = share
            payload[z, half:] = counts
        masked = jnp.where(
            mask, thrice((keys * jnp.exp(-prefix)).T, recept * jnp.exp(prefix)), 0.0
        )
        scores[...] = masked.astype(bf16)
        own = jnp.sum(recept * (column(extra[...]) + 1.0) * keys, axis=0, keepdims=True)
        local[...] = thrice(val, masked) + own * val
        by_frame = tutor[...].astype(f32).T.astype(bf16)
        tiles = GRID["x"] * GRID["core"]
        part = length // tiles
        for i in range(tiles):
            held[i] = fold(by_frame[i * part : (i + 1) * part])
        place = lax.axis_index("x")
        for s, out in enumerate((t0, t1, t2, t3)):
            to = lax.rem(place + s, GRID["x"])
            for c in range(2):
                out[c] = held[to * 2 + c]


def decays(everyone, rate, z, length):
    half = LANES // 2
    total = everyone[z, half : half + 1].astype(f32) * COUNT_BASE + everyone[
        z, half + 1 : half + 2
    ].astype(f32)
    return jnp.exp(rate * float(length) + log_half * total)


def folded_rates(codes_row, all_frames):
    return fold(jnp.broadcast_to(rates(codes_row, all_frames), (LANES, LANES)))


def yields_kernel(all_frames, everyone, local, reads, logs, codes, gain, sent, start, unit, inverse):
    length = local.shape[1]
    mine = lax.axis_index("ctx")
    half = LANES // 2
    rate = folded_rates(codes[...], all_frames)
    state = jnp.zeros((half, 2 * LANES), f32)
    for z in range(everyone.shape[0] - 1):
        longer = decays(everyone, rate, z, length) * state + everyone[z, :half].astype(f32)
        state = jnp.where(z < mine, longer, state)
    begin = unfold(state)
    start[...] = begin
    y = local[...] + thrice(begin.T, reads[...] * jnp.exp(logs[...]))
    centred = y - over_channels(y)
    inv = lax.rsqrt(over_channels(centred * centred) + epsilon)
    inverse[...] = inv
    unit[...] = centred * inv
    normed = (centred * inv * column(gain[...])).T.astype(bf16)
    tiles = GRID["x"] * GRID["core"]
    part = length // tiles
    for i in range(tiles):
        block = fold(normed[i * part : (i + 1) * part])
        for j in range(GRID["y"]):
            sent[j * tiles + i] = block


def spread(blocks):
    cols = []
    for a, b in zip(blocks[::2], blocks[1::2]):
        cols.append(
            jnp.concatenate(
                [
                    jnp.concatenate([a[:, :LANES], b[:, :LANES]], axis=1),
                    jnp.concatenate([a[:, LANES:], b[:, LANES:]], axis=1),
                ],
                axis=0,
            )
        )
    return jnp.concatenate(cols, axis=1)


def by_source(mine, other, x, c):
    step = lax.rem(lax.axis_index("x") - x + GRID["x"], GRID["x"])
    core = lax.axis_index("core")
    return jnp.where(core == c, mine[step, core], other[step, core])


def middle_kernel(
    got, t_mine, t_other, w0, w1, w2, w3, v0, v1, v2, v3, sent, m0, m1, m2, m3, held, weights, sems
):
    copies = []
    for n, source in enumerate((w0, v0, w1, v1, w2, v2, w3, v3)):
        copies.append(pltpu.make_async_copy(source, weights.at[n], sems.at[n]))
        copies[n].start()
    at, core = lax.axis_index("x"), lax.axis_index("core")
    tiles = GRID["x"] * GRID["core"]
    rows = GRID["y"]
    group = min(4, rows)
    chunks = []
    for s in range(GRID["x"]):
        x = lax.rem(at - s + GRID["x"], GRID["x"])
        for n, c in ((2 * s, core), (2 * s + 1, 1 - core)):
            for y in range(0, rows, group):
                chunks.append((n, y, [(y + g) * tiles + x * 2 + c for g in range(group)]))
    acc = None
    for n, y, places in chunks:
        if y == 0:
            copies[n].wait()
        part = weights[n, y : y + group].reshape(group * LANES, tiles * LANES)
        term = jnp.dot(spread([got[p] for p in places]), part, preferred_element_type=f32)
        acc = term if acc is None else acc + term
    mixed = acc.astype(bf16)
    for i in range(tiles):
        held[i] = fold(mixed[:, i * LANES : (i + 1) * LANES])
    for s, out in enumerate((m0, m1, m2, m3)):
        to = lax.rem(at + s, GRID["x"])
        for c in range(2):
            out[c] = held[to * 2 + c]
    wanted = spread([by_source(t_mine, t_other, i // 2, i % 2) for i in range(tiles)])
    diff = (mixed.astype(f32) - wanted.astype(f32)).astype(bf16)
    for n, y, places in chunks:
        part = weights[n, y : y + group].reshape(group * LANES, tiles * LANES)
        grads = lax.dot_general(
            part, diff, (((1,), (1,)), ((), ())), preferred_element_type=f32
        ).astype(bf16)
        for g, p in enumerate(places):
            sent[p] = fold(grads[g * LANES : (g + 1) * LANES])


def back_kernel(got, unit, inverse, gain, reads, logs, payload, sensitivity):
    tiles = GRID["x"] * GRID["core"]
    frames = []
    for i in range(tiles):
        total = got[i].astype(f32)
        for j in range(1, GRID["y"]):
            total = total + got[j * tiles + i].astype(f32)
        frames.append(unfold(total))
    scaled = jnp.concatenate(frames, axis=1) * column(gain[...])
    each = unit[...]
    grad = inverse[...] * (
        scaled - over_channels(scaled) - each * over_channels(scaled * each)
    )
    sensitivity[...] = grad
    share = fold(once(reads[...] * jnp.exp(logs[...]), grad, ((1,), (1,)))).astype(bf16)
    for z in range(payload.shape[0]):
        payload[z] = share


def window_kernel(
    m_mine, m_other, reads, keys_raw, values, logs, extra, scores, start, sensitivity,
    mixed_out, grad_reads, part_keys, part_values,
):
    length = reads.shape[1]
    tiles = GRID["x"] * GRID["core"]
    mixed_out[...] = (
        jnp.concatenate(
            [
                unfold(by_source(m_mine, m_other, i // 2, i % 2).astype(f32))
                for i in range(tiles)
            ],
            axis=0,
        ).T.astype(bf16)
    )
    recept, val, grad = reads[...], values[...], sensitivity[...]
    keys, _ = key_norm(keys_raw[...])
    prefix = logs[...]
    grow, shrink = jnp.exp(prefix), jnp.exp(-prefix)
    own_weight = column(extra[...]) + 1.0
    twofold = jnp.where(earlier(length), once(val.T, grad, ((1,), (0,))), 0.0).astype(bf16)
    progressive = jnp.sum(grad * val, axis=0, keepdims=True) * own_weight
    own = jnp.sum(recept * own_weight * keys, axis=0, keepdims=True)
    grad_reads[...] = (
        grow * (once(start[...], grad, ((1,), (0,))) + once(keys * shrink, twofold, ((1,), (0,)))) + progressive * keys
    ).astype(bf16)
    part_keys[...] = shrink * once(recept * grow, twofold, ((1,), (1,))) + progressive * recept
    part_values[...] = once(grad, scores[...], ((1,), (1,))) + own * grad


def final_kernel(
    all_frames, later, everyone, part_keys, part_values, keys_raw, values, logs, codes,
    grad_keys, grad_values,
):
    length = keys_raw.shape[1]
    mine = lax.axis_index("ctx")
    half = LANES // 2
    rate = folded_rates(codes[...], all_frames)
    state = jnp.zeros((half, 2 * LANES), f32)
    for z in range(everyone.shape[0] - 1, 0, -1):
        longer = decays(everyone, rate, z, length) * state + later[z].astype(f32)
        state = jnp.where(z > mine, longer, state)
    walking = unfold(state)
    raw = keys_raw[...]
    keys, scale = key_norm(raw)
    prefix = logs[...]
    closing = jnp.exp(prefix[:, length - 1 :] - prefix)
    grad = part_keys[...] + closing * once(walking, values[...], ((1,), (0,)))
    grad_values[...] = (part_values[...] + once(walking.T, keys * closing, ((1,), (0,)))).astype(bf16)
    grad_keys[...] = (
        0.125 * scale * (grad - scale * scale * raw * over_channels(raw * grad))
    ).astype(bf16)


def call(kernel, outs, args, here=(), cost=1 << 23, **more):
    return pl.pallas_call(
        kernel,
        cost_estimate=pl.CostEstimate(flops=1 << 30, transcendentals=0, bytes_accessed=cost),
        out_shape=[
            pltpu.VMEM(shape, kind) if n in here else jax.ShapeDtypeStruct(shape, kind)
            for n, (shape, kind) in enumerate(outs)
        ],
        **more,
    )(*args)


def near(*arrays):
    return tuple(pltpu.with_memory_space_constraint(a, pltpu.VMEM) for a in arrays)


def exchange(array, axis):
    return lax.all_to_all(array, axis, 0, 0)


def along_x(parts):
    n = GRID["x"]
    return parts[:1] + [
        lax.ppermute(parts[s], "x", [(i, (i + s) % n) for i in range(n)]) for s in range(1, n)
    ]


def swap(array):
    return lax.ppermute(array, "core", [(0, 1), (1, 0)])


def on_device(
    incoming_signals,
    receptor_linear_map,
    lock_linear_map,
    worth_linear_map,
    outbound_linear_map,
    selfward_extra,
    cluster_amplify_level,
    dwindle_powers,
    bisect_indicators,
    tutor_aggregated,
):
    length, width = incoming_signals.shape
    blocks = lax.axis_size("ctx")
    tiles, rows = GRID["x"] * GRID["core"], GRID["y"]
    part = length // tiles
    all_frames = length * blocks
    half = LANES // 2
    head = tuple(GRID)
    flat = (LANES, length)
    block = (part // 2, 2 * LANES)
    barrier = lax.optimization_barrier

    columns = exchange(
        outbound_linear_map.reshape(LANES, rows, tiles * LANES).transpose(1, 0, 2), "y"
    )

    codes = dwindle_powers.reshape(1, LANES)
    extra = selfward_extra.reshape(1, LANES)
    gain = cluster_amplify_level.reshape(1, LANES)
    halvings = bisect_indicators.reshape(1, length)

    depth = width // STEPS
    whole = pl.BlockSpec(memory_space=pltpu.VMEM)
    by_step = [
        pl.BlockSpec((length, depth), lambda k: (0, k)),
        pl.BlockSpec((LANES, depth), lambda k: (0, k)),
    ]
    payload, reads, keys_raw, values, logs, scores, local, *tutor = call(
        functools.partial(project_kernel, all_frames),
        [
            ((blocks, half + 16, 2 * LANES), bf16), (flat, f32), (flat, f32), (flat, f32),
            (flat, f32), ((length, length), bf16), (flat, f32),
        ]
        + [((2,) + block, bf16)] * GRID["x"],
        (
            incoming_signals, receptor_linear_map.T, lock_linear_map.T, worth_linear_map.T,
            codes, halvings, extra, tutor_aggregated.T,
        ),
        here=(1, 4, 6),
        grid=(STEPS,),
        in_specs=[by_step[0]] + [by_step[1]] * 3 + [whole] * 4,
        out_specs=[whole] * (7 + GRID["x"]),
        scratch_shapes=[
            pltpu.VMEM((length, 3 * LANES), f32), pltpu.VMEM((tiles,) + block, bf16),
        ],
    )
    tutor = jnp.stack(along_x(tutor))
    payload, columns, tutor = barrier((payload, columns, tutor))
    everyone = exchange(payload, "ctx")
    w_mine = along_x([columns] * GRID["x"])
    sent, start, unit, inverse = call(
        functools.partial(yields_kernel, all_frames),
        [((rows * tiles,) + block, bf16), ((LANES, LANES), f32), (flat, f32), ((1, length), f32)],
        near(everyone, local, reads, logs) + (codes, gain),
        here=(2, 3),
    )
    got = exchange(sent, head)
    w_other = [swap(w) for w in w_mine]
    sent, *mixed = call(
        middle_kernel,
        [((rows * tiles,) + block, bf16)] + [((2,) + block, bf16)] * GRID["x"],
        near(got, tutor, swap(tutor)) + (*w_mine, *w_other),
        in_specs=[whole] * 3 + [pl.BlockSpec(memory_space=pl.ANY)] * (2 * GRID["x"]),
        scratch_shapes=[
            pltpu.VMEM((tiles,) + block, bf16),
            pltpu.VMEM((2 * GRID["x"], rows, LANES, tiles * LANES), bf16),
            pltpu.SemaphoreType.DMA((2 * GRID["x"],)),
        ],
    )
    got = exchange(sent, head)
    mixed = jnp.stack(along_x(mixed))
    payload, sensitivity = call(
        back_kernel,
        [((blocks, half, 2 * LANES), bf16), (flat, f32)],
        near(got, unit, inverse) + (gain,) + near(reads, logs),
    )
    later = exchange(payload, "ctx")
    mixed_out, grad_reads, part_keys, part_values = call(
        window_kernel,
        [(flat, bf16), (flat, bf16), (flat, f32), (flat, f32)],
        (mixed, swap(mixed), reads, keys_raw, values, logs, extra, scores, start, sensitivity),
        here=(2, 3),
    )
    grad_keys, grad_values = call(
        functools.partial(final_kernel, all_frames),
        [(flat, bf16), (flat, bf16)],
        near(later, everyone, part_keys, part_values, keys_raw, values, logs) + (codes,),
    )
    return (mixed_out.T, grad_reads.T, grad_keys.T, grad_values.T)


def solution(mesh):
    blocks = mesh.shape["ctx"]
    grid = Mesh(mesh.devices.reshape((blocks,) + tuple(GRID.values())), ("ctx",) + tuple(GRID))
    head = tuple(GRID)
    in_specs = (
        P("ctx", None),
        P(None, head),
        P(None, head),
        P(None, head),
        P(head, None),
        P(head),
        P(head),
        P(head),
        P("ctx"),
        P("ctx", head),
    )
    out_specs = (P("ctx", head), P("ctx", head), P("ctx", head), P("ctx", head))
    return jax.shard_map(
        on_device, mesh=grid, in_specs=in_specs, out_specs=out_specs, check_vma=False
    )
```

```python
import functools

import jax
import jax.numpy as jnp
from jax import lax
from jax.experimental import pallas as pl
from jax.experimental.pallas import tpu as pltpu
from jax.sharding import Mesh, PartitionSpec as P

LANES = 64
CODES = 64
GRID = {"y": 8, "x": 4, "core": 2}
STEPS = 4
COUNT_BASE = 64

epsilon = 1e-05
log_half = -0.6931471805599453
rate_span = 1.2
f32 = jnp.float32
bf16 = jnp.bfloat16


def once(a, b, dims):
    return lax.dot_general(
        a.astype(bf16), b.astype(bf16), (dims, ((), ())), preferred_element_type=f32
    )


def split(a):
    high = a.astype(bf16)
    return high, (a - high.astype(f32)).astype(bf16)


def thrice(a, b):
    (a_high, a_low), (b_high, b_low) = split(a), split(b)
    if a.shape[1] <= LANES:
        return once(
            jnp.concatenate([a_high, a_high, a_low], axis=1),
            jnp.concatenate([b_high, b_low, b_high], axis=0),
            ((1,), (0,)),
        )
    both = once(jnp.concatenate([a_high, a_low], axis=0), b_high, ((1,), (0,)))
    rows = a.shape[0]
    return both[:rows] + both[rows:] + once(a_high, b_low, ((1,), (0,)))


def column(row):
    n = row.shape[1]
    at = lax.broadcasted_iota(jnp.int32, (n, n), 0)
    on = at == lax.broadcasted_iota(jnp.int32, (n, n), 1)
    return jnp.sum(jnp.where(on, row, 0.0), axis=1, keepdims=True)


def rates(codes_row, all_frames):
    return -rate_span * (column(codes_row.astype(f32)) + 1.0) / float(CODES * all_frames)


def over_channels(array):
    return jnp.mean(array, axis=0, keepdims=True)


def key_norm(keys_raw):
    scale = lax.rsqrt(over_channels(keys_raw * keys_raw) + epsilon)
    return keys_raw * scale * 0.125, scale


def fold(square):
    half = square.shape[0] // 2
    return jnp.concatenate([square[:half], square[half:]], axis=1)


def beside(block):
    half = block.shape[0] // 2
    return jnp.concatenate([block[:half], block[half:]], axis=1)


def unfold(packed):
    return jnp.concatenate([packed[:, :LANES], packed[:, LANES:]], axis=0)


def earlier(length):
    s = lax.broadcasted_iota(jnp.int32, (length, length), 0)
    return s < lax.broadcasted_iota(jnp.int32, (length, length), 1)


def project_kernel(
    all_frames, x, wr, wk, wv, codes, halvings, extra, tutor,
    payload, reads, keys_raw, values, logs, scores, local, t0, t1, t2, t3, acc, held,
):
    step = pl.program_id(0)

    @pl.when(step == 0)
    def _():
        acc[...] = jnp.zeros_like(acc)

    acc[...] += lax.dot_general(
        x[...],
        jnp.concatenate([wr[...], wk[...], wv[...]], axis=0),
        (((1,), (1,)), ((), ())),
        preferred_element_type=f32,
    )

    @pl.when(step == STEPS - 1)
    def _():
        length = x.shape[0]
        whole = acc[...].T
        recept, raw, val = whole[:LANES], whole[LANES : 2 * LANES], whole[2 * LANES :]
        reads[...] = recept
        keys_raw[...] = raw
        values[...] = val
        keys, _ = key_norm(raw)
        rate = rates(codes[...], all_frames)
        marks = jnp.broadcast_to(halvings[...].astype(f32).astype(bf16), (16, length))
        mask = earlier(length)
        ones = jnp.where(mask, 1.0, 0.0).astype(bf16)
        counted = (jnp.dot(marks, ones, preferred_element_type=f32) + marks.astype(f32))[:1]
        at = (lax.broadcasted_iota(jnp.int32, (1, length), 1) + 1).astype(f32)
        prefix = rate * at + log_half * counted
        logs[...] = prefix
        total = counted[:, length - 1 :]
        closing = jnp.exp(rate * float(length) + log_half * total - prefix)
        share = fold(once(keys * closing, val, ((1,), (1,)))).astype(bf16)
        high = jnp.floor(total * (1.0 / COUNT_BASE))
        low = total - high * COUNT_BASE
        top = lax.broadcasted_iota(jnp.int32, (16, 2 * LANES), 0) == 0
        counts = jnp.where(top, high, low).astype(bf16)
        half = LANES // 2
        for z in range(payload.shape[0]):
            payload[z, :half] = share
            payload[z, half:] = counts
        masked = jnp.where(
            mask, thrice((keys * jnp.exp(-prefix)).T, recept * jnp.exp(prefix)), 0.0
        )
        scores[...] = masked.astype(bf16)
        own = jnp.sum(recept * (column(extra[...]) + 1.0) * keys, axis=0, keepdims=True)
        local[...] = thrice(val, masked) + own * val
        by_frame = tutor[...].astype(f32).T.astype(bf16)
        tiles = GRID["x"] * GRID["core"]
        part = length // tiles
        for i in range(tiles):
            held[i] = fold(by_frame[i * part : (i + 1) * part])
        place = lax.axis_index("x")
        for s, out in enumerate((t0, t1, t2, t3)):
            to = lax.rem(place + s, GRID["x"])
            out[...] = jnp.concatenate([beside(held[to * 2 + c]) for c in range(2)], axis=1)


def decays(everyone, rate, z, length):
    half = LANES // 2
    total = everyone[z, half : half + 1].astype(f32) * COUNT_BASE + everyone[
        z, half + 1 : half + 2
    ].astype(f32)
    return jnp.exp(rate * float(length) + log_half * total)


def folded_rates(codes_row, all_frames):
    return fold(jnp.broadcast_to(rates(codes_row, all_frames), (LANES, LANES)))


def yields_kernel(all_frames, everyone, local, reads, logs, codes, gain, sent, start, unit, inverse):
    length = local.shape[1]
    mine = lax.axis_index("ctx")
    half = LANES // 2
    rate = folded_rates(codes[...], all_frames)
    state = jnp.zeros((half, 2 * LANES), f32)
    for z in range(everyone.shape[0] - 1):
        longer = decays(everyone, rate, z, length) * state + everyone[z, :half].astype(f32)
        state = jnp.where(z < mine, longer, state)
    begin = unfold(state)
    start[...] = begin
    y = local[...] + thrice(begin.T, reads[...] * jnp.exp(logs[...]))
    centred = y - over_channels(y)
    inv = lax.rsqrt(over_channels(centred * centred) + epsilon)
    inverse[...] = inv
    unit[...] = centred * inv
    normed = (centred * inv * column(gain[...])).T.astype(bf16)
    tiles = GRID["x"] * GRID["core"]
    part = length // tiles
    for i in range(tiles):
        block = fold(normed[i * part : (i + 1) * part])
        for j in range(GRID["y"]):
            sent[j * tiles + i] = block


def spread(blocks):
    cols = []
    for a, b in zip(blocks[::2], blocks[1::2]):
        cols.append(
            jnp.concatenate(
                [
                    jnp.concatenate([a[:, :LANES], b[:, :LANES]], axis=1),
                    jnp.concatenate([a[:, LANES:], b[:, LANES:]], axis=1),
                ],
                axis=0,
            )
        )
    return jnp.concatenate(cols, axis=1)


def pack_kernel(columns, t0, t1, t2, t3, p0, p1, p2, p3):
    rows = columns.shape[0] * columns.shape[1]
    matrix = columns[...].reshape(rows, columns.shape[2])
    for out, teacher in ((p0, t0), (p1, t1), (p2, t2), (p3, t3)):
        out[:rows] = matrix
        out[rows:] = teacher[...]


def by_source(mine, other, x, c):
    step = lax.rem(lax.axis_index("x") - x + GRID["x"], GRID["x"])
    core = lax.axis_index("core")
    return jnp.where(core == c, mine[step, core], other[step, core])


def middle_kernel(got, w0, w1, w2, w3, v0, v1, v2, v3, sent, m0, m1, m2, m3, held, weights, sems):
    copies = []
    for n, source in enumerate((w0, v0, w1, v1, w2, v2, w3, v3)):
        copies.append(pltpu.make_async_copy(source, weights.at[n], sems.at[n]))
        copies[n].start()
    at, core = lax.axis_index("x"), lax.axis_index("core")
    tiles = GRID["x"] * GRID["core"]
    rows = GRID["y"]
    group = min(4, rows)
    chunks = []
    for s in range(GRID["x"]):
        x = lax.rem(at - s + GRID["x"], GRID["x"])
        for n, c in ((2 * s, core), (2 * s + 1, 1 - core)):
            for y in range(0, rows, group):
                chunks.append((n, y, [(y + g) * tiles + x * 2 + c for g in range(group)]))
    acc = None
    for n, y, places in chunks:
        if y == 0:
            copies[n].wait()
        part = weights[n, y * LANES : (y + group) * LANES]
        term = jnp.dot(spread([got[p] for p in places]), part, preferred_element_type=f32)
        acc = term if acc is None else acc + term
    mixed = acc.astype(bf16)
    for i in range(tiles):
        held[i] = fold(mixed[:, i * LANES : (i + 1) * LANES])
    for s, out in enumerate((m0, m1, m2, m3)):
        to = lax.rem(at + s, GRID["x"])
        for c in range(2):
            out[c] = held[to * 2 + c]
    teachers = []
    for i in range(tiles):
        step = lax.rem(at - i // 2 + GRID["x"], GRID["x"])
        came = weights[2 * step + jnp.where(core == i % 2, 0, 1), rows * LANES :]
        wide = came.shape[1] // 2
        mine = jnp.where(core == 0, came[:, :wide], came[:, wide:])
        teachers.append(jnp.concatenate([mine[:, : wide // 2], mine[:, wide // 2 :]], axis=0))
    wanted = spread(teachers)
    diff = (mixed.astype(f32) - wanted.astype(f32)).astype(bf16)
    for n, y, places in chunks:
        part = weights[n, y * LANES : (y + group) * LANES]
        grads = lax.dot_general(
            part, diff, (((1,), (1,)), ((), ())), preferred_element_type=f32
        ).astype(bf16)
        for g, p in enumerate(places):
            sent[p] = fold(grads[g * LANES : (g + 1) * LANES])


def back_kernel(got, unit, inverse, gain, reads, logs, payload, sensitivity):
    tiles = GRID["x"] * GRID["core"]
    frames = []
    for i in range(tiles):
        total = got[i].astype(f32)
        for j in range(1, GRID["y"]):
            total = total + got[j * tiles + i].astype(f32)
        frames.append(unfold(total))
    scaled = jnp.concatenate(frames, axis=1) * column(gain[...])
    each = unit[...]
    grad = inverse[...] * (
        scaled - over_channels(scaled) - each * over_channels(scaled * each)
    )
    sensitivity[...] = grad
    share = fold(once(reads[...] * jnp.exp(logs[...]), grad, ((1,), (1,)))).astype(bf16)
    for z in range(payload.shape[0]):
        payload[z] = share


def window_kernel(
    m_mine, m_other, reads, keys_raw, values, logs, extra, scores, start, sensitivity,
    mixed_out, grad_reads, part_keys, part_values,
):
    length = reads.shape[1]
    tiles = GRID["x"] * GRID["core"]
    mixed_out[...] = (
        jnp.concatenate(
            [
                unfold(by_source(m_mine, m_other, i // 2, i % 2).astype(f32))
                for i in range(tiles)
            ],
            axis=0,
        ).T.astype(bf16)
    )
    recept, val, grad = reads[...], values[...], sensitivity[...]
    keys, _ = key_norm(keys_raw[...])
    prefix = logs[...]
    grow, shrink = jnp.exp(prefix), jnp.exp(-prefix)
    own_weight = column(extra[...]) + 1.0
    twofold = jnp.where(earlier(length), once(val.T, grad, ((1,), (0,))), 0.0).astype(bf16)
    progressive = jnp.sum(grad * val, axis=0, keepdims=True) * own_weight
    own = jnp.sum(recept * own_weight * keys, axis=0, keepdims=True)
    grad_reads[...] = (
        grow * (once(start[...], grad, ((1,), (0,))) + once(keys * shrink, twofold, ((1,), (0,)))) + progressive * keys
    ).astype(bf16)
    part_keys[...] = shrink * once(recept * grow, twofold, ((1,), (1,))) + progressive * recept
    part_values[...] = once(grad, scores[...], ((1,), (1,))) + own * grad


def final_kernel(
    all_frames, later, everyone, part_keys, part_values, keys_raw, values, logs, codes,
    grad_keys, grad_values,
):
    length = keys_raw.shape[1]
    mine = lax.axis_index("ctx")
    half = LANES // 2
    rate = folded_rates(codes[...], all_frames)
    state = jnp.zeros((half, 2 * LANES), f32)
    for z in range(everyone.shape[0] - 1, 0, -1):
        longer = decays(everyone, rate, z, length) * state + later[z].astype(f32)
        state = jnp.where(z > mine, longer, state)
    walking = unfold(state)
    raw = keys_raw[...]
    keys, scale = key_norm(raw)
    prefix = logs[...]
    closing = jnp.exp(prefix[:, length - 1 :] - prefix)
    grad = part_keys[...] + closing * once(walking, values[...], ((1,), (0,)))
    grad_values[...] = (part_values[...] + once(walking.T, keys * closing, ((1,), (0,)))).astype(bf16)
    grad_keys[...] = (
        0.125 * scale * (grad - scale * scale * raw * over_channels(raw * grad))
    ).astype(bf16)


def call(kernel, outs, args, here=(), cost=1 << 23, **more):
    return pl.pallas_call(
        kernel,
        cost_estimate=pl.CostEstimate(flops=1 << 30, transcendentals=0, bytes_accessed=cost),
        out_shape=[
            pltpu.VMEM(shape, kind) if n in here else jax.ShapeDtypeStruct(shape, kind)
            for n, (shape, kind) in enumerate(outs)
        ],
        **more,
    )(*args)


def near(*arrays):
    return tuple(pltpu.with_memory_space_constraint(a, pltpu.VMEM) for a in arrays)


def far(arrays):
    return [pltpu.with_memory_space_constraint(a, pltpu.HBM) for a in arrays]


def exchange(array, axis):
    return lax.all_to_all(array, axis, 0, 0)


def along_x(parts):
    n = GRID["x"]
    return list(parts[:1]) + [
        lax.ppermute(parts[s], "x", [(i, (i + s) % n) for i in range(n)]) for s in range(1, n)
    ]


def swap(array):
    return lax.ppermute(array, "core", [(0, 1), (1, 0)])


def on_device(
    incoming_signals,
    receptor_linear_map,
    lock_linear_map,
    worth_linear_map,
    outbound_linear_map,
    selfward_extra,
    cluster_amplify_level,
    dwindle_powers,
    bisect_indicators,
    tutor_aggregated,
):
    length, width = incoming_signals.shape
    blocks = lax.axis_size("ctx")
    tiles, rows = GRID["x"] * GRID["core"], GRID["y"]
    part = length // tiles
    all_frames = length * blocks
    half = LANES // 2
    head = tuple(GRID)
    flat = (LANES, length)
    block = (part // 2, 2 * LANES)
    teacher = ((part // 4, 8 * LANES), bf16)
    barrier = lax.optimization_barrier

    columns = exchange(
        outbound_linear_map.reshape(LANES, rows, tiles * LANES).transpose(1, 0, 2), "y"
    )

    codes = dwindle_powers.reshape(1, LANES)
    extra = selfward_extra.reshape(1, LANES)
    gain = cluster_amplify_level.reshape(1, LANES)
    halvings = bisect_indicators.reshape(1, length)

    depth = width // STEPS
    whole = pl.BlockSpec(memory_space=pltpu.VMEM)
    by_step = [
        pl.BlockSpec((length, depth), lambda k: (0, k)),
        pl.BlockSpec((LANES, depth), lambda k: (0, k)),
    ]
    payload, reads, keys_raw, values, logs, scores, local, *tutor = call(
        functools.partial(project_kernel, all_frames),
        [
            ((blocks, half + 16, 2 * LANES), bf16), (flat, f32), (flat, f32), (flat, f32),
            (flat, f32), ((length, length), bf16), (flat, f32),
        ]
        + [teacher] * GRID["x"],
        (
            incoming_signals, receptor_linear_map.T, lock_linear_map.T, worth_linear_map.T,
            codes, halvings, extra, tutor_aggregated.T,
        ),
        here=(1, 4, 6),
        grid=(STEPS,),
        in_specs=[by_step[0]] + [by_step[1]] * 3 + [whole] * 4,
        out_specs=[whole] * (7 + GRID["x"]),
        scratch_shapes=[
            pltpu.VMEM((length, 3 * LANES), f32), pltpu.VMEM((tiles,) + block, bf16),
        ],
    )
    payload, columns, *tutor = barrier((payload, columns, *tutor))
    everyone = exchange(payload, "ctx")
    packed = call(
        pack_kernel,
        [((rows * LANES + teacher[0][0], tiles * LANES), bf16)] * GRID["x"],
        near(columns) + tuple(tutor),
    )
    w_mine = far(along_x(packed))
    sent, start, unit, inverse = call(
        functools.partial(yields_kernel, all_frames),
        [((rows * tiles,) + block, bf16), ((LANES, LANES), f32), (flat, f32), ((1, length), f32)],
        near(everyone, local, reads, logs) + (codes, gain),
        here=(2, 3),
    )
    got = exchange(sent, head)
    w_other = far([swap(w) for w in w_mine])
    sent, *mixed = call(
        middle_kernel,
        [((rows * tiles,) + block, bf16)] + [((2,) + block, bf16)] * GRID["x"],
        near(got) + (*w_mine, *w_other),
        in_specs=[whole] + [pl.BlockSpec(memory_space=pl.ANY)] * (2 * GRID["x"]),
        scratch_shapes=[
            pltpu.VMEM((tiles,) + block, bf16),
            pltpu.VMEM((2 * GRID["x"],) + packed[0].shape, bf16),
            pltpu.SemaphoreType.DMA((2 * GRID["x"],)),
        ],
    )
    got = exchange(sent, head)
    mixed = jnp.stack(along_x(mixed))
    payload, sensitivity = call(
        back_kernel,
        [((blocks, half, 2 * LANES), bf16), (flat, f32)],
        near(got, unit, inverse) + (gain,) + near(reads, logs),
    )
    later = exchange(payload, "ctx")
    mixed_out, grad_reads, part_keys, part_values = call(
        window_kernel,
        [(flat, bf16), (flat, bf16), (flat, f32), (flat, f32)],
        (mixed, swap(mixed), reads, keys_raw, values, logs, extra, scores, start, sensitivity),
        here=(2, 3),
    )
    grad_keys, grad_values = call(
        functools.partial(final_kernel, all_frames),
        [(flat, bf16), (flat, bf16)],
        near(later, everyone, part_keys, part_values, keys_raw, values, logs) + (codes,),
    )
    return (mixed_out.T, grad_reads.T, grad_keys.T, grad_values.T)


def solution(mesh):
    blocks = mesh.shape["ctx"]
    grid = Mesh(mesh.devices.reshape((blocks,) + tuple(GRID.values())), ("ctx",) + tuple(GRID))
    head = tuple(GRID)
    in_specs = (
        P("ctx", None),
        P(None, head),
        P(None, head),
        P(None, head),
        P(head, None),
        P(head),
        P(head),
        P(head),
        P("ctx"),
        P("ctx", head),
    )
    out_specs = (P("ctx", head), P("ctx", head), P("ctx", head), P("ctx", head))
    return jax.shard_map(
        on_device, mesh=grid, in_specs=in_specs, out_specs=out_specs, check_vma=False
    )
```

```python
import functools

import jax
import jax.numpy as jnp
from jax import lax
from jax.experimental import pallas as pl
from jax.experimental.pallas import tpu as pltpu
from jax.sharding import Mesh, PartitionSpec as P

LANES = 64
CODES = 64
GRID = {"y": 8, "x": 4, "core": 2}
STEPS = 4
COUNT_BASE = 64

epsilon = 1e-05
log_half = -0.6931471805599453
rate_span = 1.2
f32 = jnp.float32
bf16 = jnp.bfloat16


def once(a, b, dims):
    return lax.dot_general(
        a.astype(bf16), b.astype(bf16), (dims, ((), ())), preferred_element_type=f32
    )


def split(a):
    high = a.astype(bf16)
    return high, (a - high.astype(f32)).astype(bf16)


def thrice(a, b):
    (a_high, a_low), (b_high, b_low) = split(a), split(b)
    if a.shape[1] <= LANES:
        return once(
            jnp.concatenate([a_high, a_high, a_low], axis=1),
            jnp.concatenate([b_high, b_low, b_high], axis=0),
            ((1,), (0,)),
        )
    both = once(jnp.concatenate([a_high, a_low], axis=0), b_high, ((1,), (0,)))
    rows = a.shape[0]
    return both[:rows] + both[rows:] + once(a_high, b_low, ((1,), (0,)))


def column(row):
    n = row.shape[1]
    at = lax.broadcasted_iota(jnp.int32, (n, n), 0)
    on = at == lax.broadcasted_iota(jnp.int32, (n, n), 1)
    return jnp.sum(jnp.where(on, row, 0.0), axis=1, keepdims=True)


def rates(codes_row, all_frames):
    return -rate_span * (column(codes_row.astype(f32)) + 1.0) / float(CODES * all_frames)


def over_channels(array):
    return jnp.mean(array, axis=0, keepdims=True)


def key_norm(keys_raw):
    scale = lax.rsqrt(over_channels(keys_raw * keys_raw) + epsilon)
    return keys_raw * scale * 0.125, scale


def fold(square):
    half = square.shape[0] // 2
    return jnp.concatenate([square[:half], square[half:]], axis=1)


def beside(block):
    half = block.shape[0] // 2
    return jnp.concatenate([block[:half], block[half:]], axis=1)


def unfold(packed):
    return jnp.concatenate([packed[:, :LANES], packed[:, LANES:]], axis=0)


def earlier(length):
    s = lax.broadcasted_iota(jnp.int32, (length, length), 0)
    return s < lax.broadcasted_iota(jnp.int32, (length, length), 1)


def project_kernel(
    all_frames, x, wr, wk, wv, codes, halvings, extra, tutor,
    payload, reads, keys_raw, values, logs, scores, local, t0, t1, t2, t3, acc, held,
):
    step = pl.program_id(0)

    @pl.when(step == 0)
    def _():
        acc[...] = jnp.zeros_like(acc)

    acc[...] += lax.dot_general(
        x[...],
        jnp.concatenate([wr[...], wk[...], wv[...]], axis=0),
        (((1,), (1,)), ((), ())),
        preferred_element_type=f32,
    )

    @pl.when(step == STEPS - 1)
    def _():
        length = x.shape[0]
        whole = acc[...].T
        recept, raw, val = whole[:LANES], whole[LANES : 2 * LANES], whole[2 * LANES :]
        reads[...] = recept
        keys_raw[...] = raw
        values[...] = val
        keys, _ = key_norm(raw)
        rate = rates(codes[...], all_frames)
        marks = jnp.broadcast_to(halvings[...].astype(f32).astype(bf16), (16, length))
        mask = earlier(length)
        ones = jnp.where(mask, 1.0, 0.0).astype(bf16)
        counted = (jnp.dot(marks, ones, preferred_element_type=f32) + marks.astype(f32))[:1]
        at = (lax.broadcasted_iota(jnp.int32, (1, length), 1) + 1).astype(f32)
        prefix = rate * at + log_half * counted
        logs[...] = prefix
        total = counted[:, length - 1 :]
        closing = jnp.exp(rate * float(length) + log_half * total - prefix)
        share = fold(once(keys * closing, val, ((1,), (1,)))).astype(bf16)
        high = jnp.floor(total * (1.0 / COUNT_BASE))
        low = total - high * COUNT_BASE
        top = lax.broadcasted_iota(jnp.int32, (16, 2 * LANES), 0) == 0
        counts = jnp.where(top, high, low).astype(bf16)
        half = LANES // 2
        for z in range(payload.shape[0]):
            payload[z, :half] = share
            payload[z, half:] = counts
        masked = jnp.where(
            mask, thrice((keys * jnp.exp(-prefix)).T, recept * jnp.exp(prefix)), 0.0
        )
        scores[...] = masked.astype(bf16)
        own = jnp.sum(recept * (column(extra[...]) + 1.0) * keys, axis=0, keepdims=True)
        local[...] = thrice(val, masked) + own * val
        by_frame = tutor[...].astype(f32).T.astype(bf16)
        tiles = GRID["x"] * GRID["core"]
        part = length // tiles
        for i in range(tiles):
            held[i] = fold(by_frame[i * part : (i + 1) * part])
        place = lax.axis_index("x")
        for s, out in enumerate((t0, t1, t2, t3)):
            to = lax.rem(place + s, GRID["x"])
            out[...] = jnp.concatenate([beside(held[to * 2 + c]) for c in range(2)], axis=1)


def decays(everyone, rate, z, length):
    half = LANES // 2
    total = everyone[z, half : half + 1].astype(f32) * COUNT_BASE + everyone[
        z, half + 1 : half + 2
    ].astype(f32)
    return jnp.exp(rate * float(length) + log_half * total)


def folded_rates(codes_row, all_frames):
    return fold(jnp.broadcast_to(rates(codes_row, all_frames), (LANES, LANES)))


def yields_kernel(all_frames, everyone, local, reads, logs, codes, gain, sent, start, unit, inverse):
    length = local.shape[1]
    mine = lax.axis_index("ctx")
    half = LANES // 2
    rate = folded_rates(codes[...], all_frames)
    state = jnp.zeros((half, 2 * LANES), f32)
    for z in range(everyone.shape[0] - 1):
        longer = decays(everyone, rate, z, length) * state + everyone[z, :half].astype(f32)
        state = jnp.where(z < mine, longer, state)
    begin = unfold(state)
    start[...] = begin
    y = local[...] + thrice(begin.T, reads[...] * jnp.exp(logs[...]))
    centred = y - over_channels(y)
    inv = lax.rsqrt(over_channels(centred * centred) + epsilon)
    inverse[...] = inv
    unit[...] = centred * inv
    normed = (centred * inv * column(gain[...])).T.astype(bf16)
    tiles = GRID["x"] * GRID["core"]
    part = length // tiles
    for i in range(tiles):
        block = fold(normed[i * part : (i + 1) * part])
        for j in range(GRID["y"]):
            sent[j * tiles + i] = block


def spread(blocks):
    cols = []
    for a, b in zip(blocks[::2], blocks[1::2]):
        cols.append(
            jnp.concatenate(
                [
                    jnp.concatenate([a[:, :LANES], b[:, :LANES]], axis=1),
                    jnp.concatenate([a[:, LANES:], b[:, LANES:]], axis=1),
                ],
                axis=0,
            )
        )
    return jnp.concatenate(cols, axis=1)


def pack_kernel(matrix, t0, t1, t2, t3, p0, p1, p2, p3, sems):
    rows = matrix.shape[0]
    copies = []
    for out, teacher in ((p0, t0), (p1, t1), (p2, t2), (p3, t3)):
        extra = teacher.shape[0]
        taken = out.shape[0] - extra
        for source, target in (
            (matrix.at[rows - taken :], out.at[:taken]),
            (teacher, out.at[taken:]),
        ):
            copies.append(pltpu.make_async_copy(source, target, sems.at[len(copies)]))
    for copy in copies:
        copy.start()
    for copy in copies:
        copy.wait()


def by_source(mine, other, x, c):
    step = lax.rem(lax.axis_index("x") - x + GRID["x"], GRID["x"])
    core = lax.axis_index("core")
    return jnp.where(core == c, mine[step, core], other[step, core])


def middle_kernel(
    got, w0, w1, w2, w2f, w3, v0, v1, v2, v2f, v3, sent, m0, m1, m2, m3, held, weights, sems
):
    copies = []
    upper = w2f.shape[0]
    for n, first, source in (
        (0, 0, w0), (1, 0, v0), (2, 0, w1), (3, 0, v1), (6, 0, w3), (7, 0, v3),
        (4, upper, w2), (4, 0, w2f), (5, upper, v2), (5, 0, v2f),
    ):
        target = weights.at[n, first : first + source.shape[0]]
        copies.append((n, pltpu.make_async_copy(source, target, sems.at[len(copies)])))
        copies[-1][1].start()
    at, core = lax.axis_index("x"), lax.axis_index("core")
    tiles = GRID["x"] * GRID["core"]
    rows = GRID["y"]
    group = min(4, rows)
    chunks = []
    for s in (0, 1, 3, 2):
        x = lax.rem(at - s + GRID["x"], GRID["x"])
        for n, c in ((2 * s, core), (2 * s + 1, 1 - core)):
            for y in range(0, rows, group):
                chunks.append((n, y, [(y + g) * tiles + x * 2 + c for g in range(group)]))
    acc = None
    for n, y, places in chunks:
        if y == 0:
            for m, copy in copies:
                if m == n:
                    copy.wait()
        part = weights[n, y * LANES : (y + group) * LANES]
        term = jnp.dot(spread([got[p] for p in places]), part, preferred_element_type=f32)
        acc = term if acc is None else acc + term
    mixed = acc.astype(bf16)
    for i in range(tiles):
        held[i] = fold(mixed[:, i * LANES : (i + 1) * LANES])
    for s, out in enumerate((m0, m1, m2, m3)):
        to = lax.rem(at + s, GRID["x"])
        for c in range(2):
            out[c] = held[to * 2 + c]
    teachers = []
    for i in range(tiles):
        step = lax.rem(at - i // 2 + GRID["x"], GRID["x"])
        came = weights[2 * step + jnp.where(core == i % 2, 0, 1), rows * LANES :]
        wide = came.shape[1] // 2
        mine = jnp.where(core == 0, came[:, :wide], came[:, wide:])
        teachers.append(jnp.concatenate([mine[:, : wide // 2], mine[:, wide // 2 :]], axis=0))
    wanted = spread(teachers)
    diff = (mixed.astype(f32) - wanted.astype(f32)).astype(bf16)
    for n, y, places in chunks:
        part = weights[n, y * LANES : (y + group) * LANES]
        grads = lax.dot_general(
            part, diff, (((1,), (1,)), ((), ())), preferred_element_type=f32
        ).astype(bf16)
        for g, p in enumerate(places):
            sent[p] = fold(grads[g * LANES : (g + 1) * LANES])


def back_kernel(got, unit, inverse, gain, reads, logs, payload, sensitivity):
    tiles = GRID["x"] * GRID["core"]
    frames = []
    for i in range(tiles):
        total = got[i].astype(f32)
        for j in range(1, GRID["y"]):
            total = total + got[j * tiles + i].astype(f32)
        frames.append(unfold(total))
    scaled = jnp.concatenate(frames, axis=1) * column(gain[...])
    each = unit[...]
    grad = inverse[...] * (
        scaled - over_channels(scaled) - each * over_channels(scaled * each)
    )
    sensitivity[...] = grad
    share = fold(once(reads[...] * jnp.exp(logs[...]), grad, ((1,), (1,)))).astype(bf16)
    for z in range(payload.shape[0]):
        payload[z] = share


def window_kernel(
    m_mine, m_other, reads, keys_raw, values, logs, extra, scores, start, sensitivity,
    mixed_out, grad_reads, part_keys, part_values,
):
    length = reads.shape[1]
    tiles = GRID["x"] * GRID["core"]
    mixed_out[...] = (
        jnp.concatenate(
            [
                unfold(by_source(m_mine, m_other, i // 2, i % 2).astype(f32))
                for i in range(tiles)
            ],
            axis=0,
        ).T.astype(bf16)
    )
    recept, val, grad = reads[...], values[...], sensitivity[...]
    keys, _ = key_norm(keys_raw[...])
    prefix = logs[...]
    grow, shrink = jnp.exp(prefix), jnp.exp(-prefix)
    own_weight = column(extra[...]) + 1.0
    twofold = jnp.where(earlier(length), once(val.T, grad, ((1,), (0,))), 0.0).astype(bf16)
    progressive = jnp.sum(grad * val, axis=0, keepdims=True) * own_weight
    own = jnp.sum(recept * own_weight * keys, axis=0, keepdims=True)
    grad_reads[...] = (
        grow * (once(start[...], grad, ((1,), (0,))) + once(keys * shrink, twofold, ((1,), (0,)))) + progressive * keys
    ).astype(bf16)
    part_keys[...] = shrink * once(recept * grow, twofold, ((1,), (1,))) + progressive * recept
    part_values[...] = once(grad, scores[...], ((1,), (1,))) + own * grad


def final_kernel(
    all_frames, later, everyone, part_keys, part_values, keys_raw, values, logs, codes,
    grad_keys, grad_values,
):
    length = keys_raw.shape[1]
    mine = lax.axis_index("ctx")
    half = LANES // 2
    rate = folded_rates(codes[...], all_frames)
    state = jnp.zeros((half, 2 * LANES), f32)
    for z in range(everyone.shape[0] - 1, 0, -1):
        longer = decays(everyone, rate, z, length) * state + later[z].astype(f32)
        state = jnp.where(z > mine, longer, state)
    walking = unfold(state)
    raw = keys_raw[...]
    keys, scale = key_norm(raw)
    prefix = logs[...]
    closing = jnp.exp(prefix[:, length - 1 :] - prefix)
    grad = part_keys[...] + closing * once(walking, values[...], ((1,), (0,)))
    grad_values[...] = (part_values[...] + once(walking.T, keys * closing, ((1,), (0,)))).astype(bf16)
    grad_keys[...] = (
        0.125 * scale * (grad - scale * scale * raw * over_channels(raw * grad))
    ).astype(bf16)


def call(kernel, outs, args, here=(), cost=1 << 23, **more):
    return pl.pallas_call(
        kernel,
        cost_estimate=pl.CostEstimate(flops=1 << 30, transcendentals=0, bytes_accessed=cost),
        out_shape=[
            pltpu.VMEM(shape, kind) if n in here else jax.ShapeDtypeStruct(shape, kind)
            for n, (shape, kind) in enumerate(outs)
        ],
        **more,
    )(*args)


def near(*arrays):
    return tuple(pltpu.with_memory_space_constraint(a, pltpu.VMEM) for a in arrays)


def exchange(array, axis):
    return lax.all_to_all(array, axis, 0, 0)


def along_x(parts):
    n = GRID["x"]
    return list(parts[:1]) + [
        lax.ppermute(parts[s], "x", [(i, (i + s) % n) for i in range(n)]) for s in range(1, n)
    ]


def swap(array):
    return lax.ppermute(array, "core", [(0, 1), (1, 0)])


def on_device(
    incoming_signals,
    receptor_linear_map,
    lock_linear_map,
    worth_linear_map,
    outbound_linear_map,
    selfward_extra,
    cluster_amplify_level,
    dwindle_powers,
    bisect_indicators,
    tutor_aggregated,
):
    length, width = incoming_signals.shape
    blocks = lax.axis_size("ctx")
    tiles, rows = GRID["x"] * GRID["core"], GRID["y"]
    part = length // tiles
    all_frames = length * blocks
    half = LANES // 2
    head = tuple(GRID)
    flat = (LANES, length)
    block = (part // 2, 2 * LANES)
    teacher = ((part // 4, 8 * LANES), bf16)
    barrier = lax.optimization_barrier

    columns = exchange(
        outbound_linear_map.reshape(LANES, rows, tiles * LANES).transpose(1, 0, 2), "y"
    )

    codes = dwindle_powers.reshape(1, LANES)
    extra = selfward_extra.reshape(1, LANES)
    gain = cluster_amplify_level.reshape(1, LANES)
    halvings = bisect_indicators.reshape(1, length)

    depth = width // STEPS
    whole = pl.BlockSpec(memory_space=pltpu.VMEM)
    by_step = [
        pl.BlockSpec((length, depth), lambda k: (0, k)),
        pl.BlockSpec((LANES, depth), lambda k: (0, k)),
    ]
    payload, reads, keys_raw, values, logs, scores, local, *tutor = call(
        functools.partial(project_kernel, all_frames),
        [
            ((blocks, half + 16, 2 * LANES), bf16), (flat, f32), (flat, f32), (flat, f32),
            (flat, f32), ((length, length), bf16), (flat, f32),
        ]
        + [teacher] * GRID["x"],
        (
            incoming_signals, receptor_linear_map.T, lock_linear_map.T, worth_linear_map.T,
            codes, halvings, extra, tutor_aggregated.T,
        ),
        here=(1, 4, 6),
        grid=(STEPS,),
        in_specs=[by_step[0]] + [by_step[1]] * 3 + [whole] * 4,
        out_specs=[whole] * (7 + GRID["x"]),
        scratch_shapes=[
            pltpu.VMEM((length, 3 * LANES), f32), pltpu.VMEM((tiles,) + block, bf16),
        ],
    )
    payload, columns, *tutor = barrier((payload, columns, *tutor))
    everyone = exchange(payload, "ctx")
    height, upper = rows * LANES, rows * LANES // 2
    full = ((height + teacher[0][0], tiles * LANES), bf16)
    lower = ((height - upper + teacher[0][0], tiles * LANES), bf16)
    anywhere = pl.BlockSpec(memory_space=pl.ANY)
    packed = call(
        pack_kernel,
        [full, full, lower, full],
        near(columns.reshape(height, tiles * LANES)) + tuple(tutor),
        out_specs=[anywhere] * GRID["x"],
        scratch_shapes=[pltpu.SemaphoreType.DMA((2 * GRID["x"],))],
    )
    w0, w1, w2, w3 = along_x(packed)
    w2f = lax.ppermute(w3[:upper], "x", [(i, (i + 3) % GRID["x"]) for i in range(GRID["x"])])
    w_mine = [w0, w1, w2, w2f, w3]
    sent, start, unit, inverse = call(
        functools.partial(yields_kernel, all_frames),
        [((rows * tiles,) + block, bf16), ((LANES, LANES), f32), (flat, f32), ((1, length), f32)],
        near(everyone, local, reads, logs) + (codes, gain),
        here=(2, 3),
    )
    got = exchange(sent, head)
    w_other = [swap(w) for w in w_mine]
    sent, *mixed = call(
        middle_kernel,
        [((rows * tiles,) + block, bf16)] + [((2,) + block, bf16)] * GRID["x"],
        near(got) + (*w_mine, *w_other),
        in_specs=[whole] + [anywhere] * len(w_mine + w_other),
        scratch_shapes=[
            pltpu.VMEM((tiles,) + block, bf16),
            pltpu.VMEM((2 * GRID["x"],) + packed[0].shape, bf16),
            pltpu.SemaphoreType.DMA((len(w_mine + w_other),)),
        ],
    )
    got = exchange(sent, head)
    mixed = jnp.stack(along_x(mixed))
    payload, sensitivity = call(
        back_kernel,
        [((blocks, half, 2 * LANES), bf16), (flat, f32)],
        near(got, unit, inverse) + (gain,) + near(reads, logs),
    )
    later = exchange(payload, "ctx")
    mixed_out, grad_reads, part_keys, part_values = call(
        window_kernel,
        [(flat, bf16), (flat, bf16), (flat, f32), (flat, f32)],
        (mixed, swap(mixed), reads, keys_raw, values, logs, extra, scores, start, sensitivity),
        here=(2, 3),
    )
    grad_keys, grad_values = call(
        functools.partial(final_kernel, all_frames),
        [(flat, bf16), (flat, bf16)],
        near(later, everyone, part_keys, part_values, keys_raw, values, logs) + (codes,),
    )
    return (mixed_out.T, grad_reads.T, grad_keys.T, grad_values.T)


def solution(mesh):
    blocks = mesh.shape["ctx"]
    grid = Mesh(mesh.devices.reshape((blocks,) + tuple(GRID.values())), ("ctx",) + tuple(GRID))
    head = tuple(GRID)
    in_specs = (
        P("ctx", None),
        P(None, head),
        P(None, head),
        P(None, head),
        P(head, None),
        P(head),
        P(head),
        P(head),
        P("ctx"),
        P("ctx", head),
    )
    out_specs = (P("ctx", head), P("ctx", head), P("ctx", head), P("ctx", head))
    return jax.shard_map(
        on_device, mesh=grid, in_specs=in_specs, out_specs=out_specs, check_vma=False
    )
```

```python
import functools

import jax
import jax.numpy as jnp
from jax import lax
from jax.experimental import pallas as pl
from jax.experimental.pallas import tpu as pltpu
from jax.sharding import Mesh, PartitionSpec as P

LANES = 64
CODES = 64
GRID = {"y": 8, "x": 4, "core": 2}
STEPS = 4
COUNT_BASE = 64

epsilon = 1e-05
log_half = -0.6931471805599453
rate_span = 1.2
f32 = jnp.float32
bf16 = jnp.bfloat16


def once(a, b, dims):
    return lax.dot_general(
        a.astype(bf16), b.astype(bf16), (dims, ((), ())), preferred_element_type=f32
    )


def split(a):
    high = a.astype(bf16)
    return high, (a - high.astype(f32)).astype(bf16)


def thrice(a, b):
    (a_high, a_low), (b_high, b_low) = split(a), split(b)
    if a.shape[1] <= LANES:
        return once(
            jnp.concatenate([a_high, a_high, a_low], axis=1),
            jnp.concatenate([b_high, b_low, b_high], axis=0),
            ((1,), (0,)),
        )
    both = once(jnp.concatenate([a_high, a_low], axis=0), b_high, ((1,), (0,)))
    rows = a.shape[0]
    return both[:rows] + both[rows:] + once(a_high, b_low, ((1,), (0,)))


def column(row):
    n = row.shape[1]
    at = lax.broadcasted_iota(jnp.int32, (n, n), 0)
    on = at == lax.broadcasted_iota(jnp.int32, (n, n), 1)
    return jnp.sum(jnp.where(on, row, 0.0), axis=1, keepdims=True)


def rates(codes_row, all_frames):
    return -rate_span * (column(codes_row.astype(f32)) + 1.0) / float(CODES * all_frames)


def over_channels(array):
    return jnp.mean(array, axis=0, keepdims=True)


def key_norm(keys_raw):
    scale = lax.rsqrt(over_channels(keys_raw * keys_raw) + epsilon)
    return keys_raw * scale * 0.125, scale


def fold(square):
    half = square.shape[0] // 2
    return jnp.concatenate([square[:half], square[half:]], axis=1)


def beside(block):
    half = block.shape[0] // 2
    return jnp.concatenate([block[:half], block[half:]], axis=1)


def unfold(packed):
    return jnp.concatenate([packed[:, :LANES], packed[:, LANES:]], axis=0)


def earlier(length):
    s = lax.broadcasted_iota(jnp.int32, (length, length), 0)
    return s < lax.broadcasted_iota(jnp.int32, (length, length), 1)


def project_kernel(
    all_frames, x, wr, wk, wv, codes, halvings, extra, tutor,
    payload, reads, keys_raw, values, logs, scores, local, t0, t1, t2, t3, acc, held,
):
    step = pl.program_id(0)

    @pl.when(step == 0)
    def _():
        acc[...] = jnp.zeros_like(acc)

    acc[...] += lax.dot_general(
        x[...],
        jnp.concatenate([wr[...], wk[...], wv[...]], axis=0),
        (((1,), (1,)), ((), ())),
        preferred_element_type=f32,
    )

    @pl.when(step == STEPS - 1)
    def _():
        length = x.shape[0]
        whole = acc[...].T
        recept, raw, val = whole[:LANES], whole[LANES : 2 * LANES], whole[2 * LANES :]
        reads[...] = recept
        keys_raw[...] = raw
        values[...] = val
        keys, _ = key_norm(raw)
        rate = rates(codes[...], all_frames)
        marks = jnp.broadcast_to(halvings[...].astype(f32).astype(bf16), (16, length))
        mask = earlier(length)
        ones = jnp.where(mask, 1.0, 0.0).astype(bf16)
        counted = (jnp.dot(marks, ones, preferred_element_type=f32) + marks.astype(f32))[:1]
        at = (lax.broadcasted_iota(jnp.int32, (1, length), 1) + 1).astype(f32)
        prefix = rate * at + log_half * counted
        logs[...] = prefix
        total = counted[:, length - 1 :]
        closing = jnp.exp(rate * float(length) + log_half * total - prefix)
        share = fold(once(keys * closing, val, ((1,), (1,)))).astype(bf16)
        high = jnp.floor(total * (1.0 / COUNT_BASE))
        low = total - high * COUNT_BASE
        top = lax.broadcasted_iota(jnp.int32, (16, 2 * LANES), 0) == 0
        counts = jnp.where(top, high, low).astype(bf16)
        half = LANES // 2
        for z in range(payload.shape[0]):
            payload[z, :half] = share
            payload[z, half:] = counts
        masked = jnp.where(
            mask, thrice((keys * jnp.exp(-prefix)).T, recept * jnp.exp(prefix)), 0.0
        )
        scores[...] = masked.astype(bf16)
        own = jnp.sum(recept * (column(extra[...]) + 1.0) * keys, axis=0, keepdims=True)
        local[...] = thrice(val, masked) + own * val
        by_frame = tutor[...].astype(f32).T.astype(bf16)
        tiles = GRID["x"] * GRID["core"]
        part = length // tiles
        for i in range(tiles):
            held[i] = fold(by_frame[i * part : (i + 1) * part])
        place = lax.axis_index("x")
        for s, out in enumerate((t0, t1, t2, t3)):
            to = lax.rem(place + s, GRID["x"])
            out[...] = jnp.concatenate([beside(held[to * 2 + c]) for c in range(2)], axis=1)


def decays(everyone, rate, z, length):
    half = LANES // 2
    total = everyone[z, half : half + 1].astype(f32) * COUNT_BASE + everyone[
        z, half + 1 : half + 2
    ].astype(f32)
    return jnp.exp(rate * float(length) + log_half * total)


def folded_rates(codes_row, all_frames):
    return fold(jnp.broadcast_to(rates(codes_row, all_frames), (LANES, LANES)))


def yields_kernel(all_frames, everyone, local, reads, logs, codes, gain, sent, start, unit, inverse):
    length = local.shape[1]
    mine = lax.axis_index("ctx")
    half = LANES // 2
    rate = folded_rates(codes[...], all_frames)
    state = jnp.zeros((half, 2 * LANES), f32)
    for z in range(everyone.shape[0] - 1):
        longer = decays(everyone, rate, z, length) * state + everyone[z, :half].astype(f32)
        state = jnp.where(z < mine, longer, state)
    begin = unfold(state)
    start[...] = begin
    y = local[...] + thrice(begin.T, reads[...] * jnp.exp(logs[...]))
    centred = y - over_channels(y)
    inv = lax.rsqrt(over_channels(centred * centred) + epsilon)
    inverse[...] = inv
    unit[...] = centred * inv
    normed = (centred * inv * column(gain[...])).T.astype(bf16)
    tiles = GRID["x"] * GRID["core"]
    part = length // tiles
    for i in range(tiles):
        block = fold(normed[i * part : (i + 1) * part])
        for j in range(GRID["y"]):
            sent[j * tiles + i] = block


def spread(blocks):
    cols = []
    for a, b in zip(blocks[::2], blocks[1::2]):
        cols.append(
            jnp.concatenate(
                [
                    jnp.concatenate([a[:, :LANES], b[:, :LANES]], axis=1),
                    jnp.concatenate([a[:, LANES:], b[:, LANES:]], axis=1),
                ],
                axis=0,
            )
        )
    return jnp.concatenate(cols, axis=1)


def pack_kernel(columns, t0, t1, t2, t3, p0, p1, p2, p3):
    rows = columns.shape[0] * columns.shape[1]
    matrix = columns[...].reshape(rows, columns.shape[2])
    for out, teacher in ((p0, t0), (p1, t1), (p2, t2), (p3, t3)):
        out[:rows] = matrix
        out[rows:] = teacher[...]


def by_source(mine, other, x, c):
    step = lax.rem(lax.axis_index("x") - x + GRID["x"], GRID["x"])
    core = lax.axis_index("core")
    return jnp.where(core == c, mine[step, core], other[step, core])


def middle_kernel(got, w0, w1, w3, w2, v0, v1, v3, v2, sent, m0, m1, m2, m3, held, weights, sems):
    copies = []
    for n, source in enumerate((w0, v0, w1, v1, w2, v2, w3, v3)):
        copies.append(pltpu.make_async_copy(source, weights.at[n], sems.at[n]))
        copies[n].start()
    at, core = lax.axis_index("x"), lax.axis_index("core")
    tiles = GRID["x"] * GRID["core"]
    rows = GRID["y"]
    group = min(4, rows)
    chunks = []
    for s in (0, 1, 3, 2):
        x = lax.rem(at - s + GRID["x"], GRID["x"])
        for n, c in ((2 * s, core), (2 * s + 1, 1 - core)):
            for y in range(0, rows, group):
                chunks.append((n, y, [(y + g) * tiles + x * 2 + c for g in range(group)]))
    acc = None
    for n, y, places in chunks:
        if y == 0:
            copies[n].wait()
        part = weights[n, y * LANES : (y + group) * LANES]
        term = jnp.dot(spread([got[p] for p in places]), part, preferred_element_type=f32)
        acc = term if acc is None else acc + term
    mixed = acc.astype(bf16)
    for i in range(tiles):
        held[i] = fold(mixed[:, i * LANES : (i + 1) * LANES])
    for s, out in enumerate((m0, m1, m2, m3)):
        to = lax.rem(at + s, GRID["x"])
        for c in range(2):
            out[c] = held[to * 2 + c]
    teachers = []
    for i in range(tiles):
        step = lax.rem(at - i // 2 + GRID["x"], GRID["x"])
        came = weights[2 * step + jnp.where(core == i % 2, 0, 1), rows * LANES :]
        wide = came.shape[1] // 2
        mine = jnp.where(core == 0, came[:, :wide], came[:, wide:])
        teachers.append(jnp.concatenate([mine[:, : wide // 2], mine[:, wide // 2 :]], axis=0))
    wanted = spread(teachers)
    diff = (mixed.astype(f32) - wanted.astype(f32)).astype(bf16)
    for n, y, places in chunks:
        part = weights[n, y * LANES : (y + group) * LANES]
        grads = lax.dot_general(
            part, diff, (((1,), (1,)), ((), ())), preferred_element_type=f32
        ).astype(bf16)
        for g, p in enumerate(places):
            sent[p] = fold(grads[g * LANES : (g + 1) * LANES])


def back_kernel(got, unit, inverse, gain, reads, logs, payload, sensitivity):
    tiles = GRID["x"] * GRID["core"]
    frames = []
    for i in range(tiles):
        total = got[i].astype(f32)
        for j in range(1, GRID["y"]):
            total = total + got[j * tiles + i].astype(f32)
        frames.append(unfold(total))
    scaled = jnp.concatenate(frames, axis=1) * column(gain[...])
    each = unit[...]
    grad = inverse[...] * (
        scaled - over_channels(scaled) - each * over_channels(scaled * each)
    )
    sensitivity[...] = grad
    share = fold(once(reads[...] * jnp.exp(logs[...]), grad, ((1,), (1,)))).astype(bf16)
    for z in range(payload.shape[0]):
        payload[z] = share


def window_kernel(
    m_mine, m_other, reads, keys_raw, values, logs, extra, scores, start, sensitivity,
    mixed_out, grad_reads, part_keys, part_values,
):
    length = reads.shape[1]
    tiles = GRID["x"] * GRID["core"]
    mixed_out[...] = (
        jnp.concatenate(
            [
                unfold(by_source(m_mine, m_other, i // 2, i % 2).astype(f32))
                for i in range(tiles)
            ],
            axis=0,
        ).T.astype(bf16)
    )
    recept, val, grad = reads[...], values[...], sensitivity[...]
    keys, _ = key_norm(keys_raw[...])
    prefix = logs[...]
    grow, shrink = jnp.exp(prefix), jnp.exp(-prefix)
    own_weight = column(extra[...]) + 1.0
    twofold = jnp.where(earlier(length), once(val.T, grad, ((1,), (0,))), 0.0).astype(bf16)
    progressive = jnp.sum(grad * val, axis=0, keepdims=True) * own_weight
    own = jnp.sum(recept * own_weight * keys, axis=0, keepdims=True)
    grad_reads[...] = (
        grow * (once(start[...], grad, ((1,), (0,))) + once(keys * shrink, twofold, ((1,), (0,)))) + progressive * keys
    ).astype(bf16)
    part_keys[...] = shrink * once(recept * grow, twofold, ((1,), (1,))) + progressive * recept
    part_values[...] = once(grad, scores[...], ((1,), (1,))) + own * grad


def final_kernel(
    all_frames, later, everyone, part_keys, part_values, keys_raw, values, logs, codes,
    grad_keys, grad_values,
):
    length = keys_raw.shape[1]
    mine = lax.axis_index("ctx")
    half = LANES // 2
    rate = folded_rates(codes[...], all_frames)
    state = jnp.zeros((half, 2 * LANES), f32)
    for z in range(everyone.shape[0] - 1, 0, -1):
        longer = decays(everyone, rate, z, length) * state + later[z].astype(f32)
        state = jnp.where(z > mine, longer, state)
    walking = unfold(state)
    raw = keys_raw[...]
    keys, scale = key_norm(raw)
    prefix = logs[...]
    closing = jnp.exp(prefix[:, length - 1 :] - prefix)
    grad = part_keys[...] + closing * once(walking, values[...], ((1,), (0,)))
    grad_values[...] = (part_values[...] + once(walking.T, keys * closing, ((1,), (0,)))).astype(bf16)
    grad_keys[...] = (
        0.125 * scale * (grad - scale * scale * raw * over_channels(raw * grad))
    ).astype(bf16)


def call(kernel, outs, args, here=(), cost=1 << 23, **more):
    return pl.pallas_call(
        kernel,
        cost_estimate=pl.CostEstimate(flops=1 << 30, transcendentals=0, bytes_accessed=cost),
        out_shape=[
            pltpu.VMEM(shape, kind) if n in here else jax.ShapeDtypeStruct(shape, kind)
            for n, (shape, kind) in enumerate(outs)
        ],
        **more,
    )(*args)


def near(*arrays):
    return tuple(pltpu.with_memory_space_constraint(a, pltpu.VMEM) for a in arrays)


def exchange(array, axis):
    return lax.all_to_all(array, axis, 0, 0)


def along_x(parts):
    n = GRID["x"]
    came = {
        s: lax.ppermute(parts[s], "x", [(i, (i + s) % n) for i in range(n)]) for s in (1, 3, 2)
    }
    return [parts[0], came[1], came[2], came[3]]


def swap(array):
    return lax.ppermute(array, "core", [(0, 1), (1, 0)])


def on_device(
    incoming_signals,
    receptor_linear_map,
    lock_linear_map,
    worth_linear_map,
    outbound_linear_map,
    selfward_extra,
    cluster_amplify_level,
    dwindle_powers,
    bisect_indicators,
    tutor_aggregated,
):
    length, width = incoming_signals.shape
    blocks = lax.axis_size("ctx")
    tiles, rows = GRID["x"] * GRID["core"], GRID["y"]
    part = length // tiles
    all_frames = length * blocks
    half = LANES // 2
    head = tuple(GRID)
    flat = (LANES, length)
    block = (part // 2, 2 * LANES)
    teacher = ((part // 4, 8 * LANES), bf16)
    barrier = lax.optimization_barrier

    columns = exchange(
        outbound_linear_map.reshape(LANES, rows, tiles * LANES).transpose(1, 0, 2), "y"
    )

    codes = dwindle_powers.reshape(1, LANES)
    extra = selfward_extra.reshape(1, LANES)
    gain = cluster_amplify_level.reshape(1, LANES)
    halvings = bisect_indicators.reshape(1, length)

    depth = width // STEPS
    whole = pl.BlockSpec(memory_space=pltpu.VMEM)
    by_step = [
        pl.BlockSpec((length, depth), lambda k: (0, k)),
        pl.BlockSpec((LANES, depth), lambda k: (0, k)),
    ]
    payload, reads, keys_raw, values, logs, scores, local, *tutor = call(
        functools.partial(project_kernel, all_frames),
        [
            ((blocks, half + 16, 2 * LANES), bf16), (flat, f32), (flat, f32), (flat, f32),
            (flat, f32), ((length, length), bf16), (flat, f32),
        ]
        + [teacher] * GRID["x"],
        (
            incoming_signals, receptor_linear_map.T, lock_linear_map.T, worth_linear_map.T,
            codes, halvings, extra, tutor_aggregated.T,
        ),
        here=(1, 4, 6),
        grid=(STEPS,),
        in_specs=[by_step[0]] + [by_step[1]] * 3 + [whole] * 4,
        out_specs=[whole] * (7 + GRID["x"]),
        scratch_shapes=[
            pltpu.VMEM((length, 3 * LANES), f32), pltpu.VMEM((tiles,) + block, bf16),
        ],
    )
    payload, columns, *tutor = barrier((payload, columns, *tutor))
    everyone = exchange(payload, "ctx")
    packed = call(
        pack_kernel,
        [((rows * LANES + teacher[0][0], tiles * LANES), bf16)] * GRID["x"],
        near(columns) + tuple(tutor),
    )
    w_mine = along_x(packed)
    sent, start, unit, inverse = call(
        functools.partial(yields_kernel, all_frames),
        [((rows * tiles,) + block, bf16), ((LANES, LANES), f32), (flat, f32), ((1, length), f32)],
        near(everyone, local, reads, logs) + (codes, gain),
        here=(2, 3),
    )
    got = exchange(sent, head)
    other = {s: swap(w_mine[s]) for s in (0, 1, 3, 2)}
    w_other = [other[s] for s in (0, 1, 3, 2)]
    w_mine = [w_mine[s] for s in (0, 1, 3, 2)]
    sent, *mixed = call(
        middle_kernel,
        [((rows * tiles,) + block, bf16)] + [((2,) + block, bf16)] * GRID["x"],
        near(got) + (*w_mine,) + near(w_other[0]) + (*w_other[1:],),
        in_specs=[whole]
        + [pl.BlockSpec(memory_space=pl.ANY)] * GRID["x"]
        + [whole]
        + [pl.BlockSpec(memory_space=pl.ANY)] * (GRID["x"] - 1),
        scratch_shapes=[
            pltpu.VMEM((tiles,) + block, bf16),
            pltpu.VMEM((2 * GRID["x"],) + packed[0].shape, bf16),
            pltpu.SemaphoreType.DMA((2 * GRID["x"],)),
        ],
    )
    got = exchange(sent, head)
    mixed = jnp.stack(along_x(mixed))
    payload, sensitivity = call(
        back_kernel,
        [((blocks, half, 2 * LANES), bf16), (flat, f32)],
        near(got, unit, inverse) + (gain,) + near(reads, logs),
    )
    later = exchange(payload, "ctx")
    mixed_out, grad_reads, part_keys, part_values = call(
        window_kernel,
        [(flat, bf16), (flat, bf16), (flat, f32), (flat, f32)],
        (mixed, swap(mixed), reads, keys_raw, values, logs, extra, scores, start, sensitivity),
        here=(2, 3),
    )
    grad_keys, grad_values = call(
        functools.partial(final_kernel, all_frames),
        [(flat, bf16), (flat, bf16)],
        near(later, everyone, part_keys, part_values, keys_raw, values, logs) + (codes,),
    )
    return (mixed_out.T, grad_reads.T, grad_keys.T, grad_values.T)


def solution(mesh):
    blocks = mesh.shape["ctx"]
    grid = Mesh(mesh.devices.reshape((blocks,) + tuple(GRID.values())), ("ctx",) + tuple(GRID))
    head = tuple(GRID)
    in_specs = (
        P("ctx", None),
        P(None, head),
        P(None, head),
        P(None, head),
        P(head, None),
        P(head),
        P(head),
        P(head),
        P("ctx"),
        P("ctx", head),
    )
    out_specs = (P("ctx", head), P("ctx", head), P("ctx", head), P("ctx", head))
    return jax.shard_map(
        on_device, mesh=grid, in_specs=in_specs, out_specs=out_specs, check_vma=False
    )
```

```python
import functools

import jax
import jax.numpy as jnp
from jax import lax
from jax.experimental import pallas as pl
from jax.experimental.pallas import tpu as pltpu
from jax.sharding import Mesh, PartitionSpec as P

LANES = 64
CODES = 64
GRID = {"y": 8, "x": 4, "core": 2}
STEPS = 4
COUNT_BASE = 64

epsilon = 1e-05
log_half = -0.6931471805599453
rate_span = 1.2
f32 = jnp.float32
bf16 = jnp.bfloat16


def once(a, b, dims):
    return lax.dot_general(
        a.astype(bf16), b.astype(bf16), (dims, ((), ())), preferred_element_type=f32
    )


def split(a):
    high = a.astype(bf16)
    return high, (a - high.astype(f32)).astype(bf16)


def thrice(a, b):
    (a_high, a_low), (b_high, b_low) = split(a), split(b)
    if a.shape[1] <= LANES:
        return once(
            jnp.concatenate([a_high, a_high, a_low], axis=1),
            jnp.concatenate([b_high, b_low, b_high], axis=0),
            ((1,), (0,)),
        )
    both = once(jnp.concatenate([a_high, a_low], axis=0), b_high, ((1,), (0,)))
    rows = a.shape[0]
    return both[:rows] + both[rows:] + once(a_high, b_low, ((1,), (0,)))


def column(row):
    n = row.shape[1]
    at = lax.broadcasted_iota(jnp.int32, (n, n), 0)
    on = at == lax.broadcasted_iota(jnp.int32, (n, n), 1)
    return jnp.sum(jnp.where(on, row, 0.0), axis=1, keepdims=True)


def rates(codes_row, all_frames):
    return -rate_span * (column(codes_row.astype(f32)) + 1.0) / float(CODES * all_frames)


def over_channels(array):
    return jnp.mean(array, axis=0, keepdims=True)


def key_norm(keys_raw):
    scale = lax.rsqrt(over_channels(keys_raw * keys_raw) + epsilon)
    return keys_raw * scale * 0.125, scale


def fold(square):
    half = square.shape[0] // 2
    return jnp.concatenate([square[:half], square[half:]], axis=1)


def beside(block):
    half = block.shape[0] // 2
    return jnp.concatenate([block[:half], block[half:]], axis=1)


def unfold(packed):
    return jnp.concatenate([packed[:, :LANES], packed[:, LANES:]], axis=0)


def earlier(length):
    s = lax.broadcasted_iota(jnp.int32, (length, length), 0)
    return s < lax.broadcasted_iota(jnp.int32, (length, length), 1)


def project_kernel(
    all_frames, x, wr, wk, wv, codes, halvings, extra, tutor,
    payload, reads, keys_raw, values, logs, scores, local, t0, t1, t2, t3, acc, held,
):
    step = pl.program_id(0)

    @pl.when(step == 0)
    def _():
        acc[...] = jnp.zeros_like(acc)

    acc[...] += lax.dot_general(
        x[...],
        jnp.concatenate([wr[...], wk[...], wv[...]], axis=0),
        (((1,), (1,)), ((), ())),
        preferred_element_type=f32,
    )

    @pl.when(step == STEPS - 1)
    def _():
        length = x.shape[0]
        whole = acc[...].T
        recept, raw, val = whole[:LANES], whole[LANES : 2 * LANES], whole[2 * LANES :]
        reads[...] = recept
        keys_raw[...] = raw
        values[...] = val
        keys, _ = key_norm(raw)
        rate = rates(codes[...], all_frames)
        marks = jnp.broadcast_to(halvings[...].astype(f32).astype(bf16), (16, length))
        mask = earlier(length)
        ones = jnp.where(mask, 1.0, 0.0).astype(bf16)
        counted = (jnp.dot(marks, ones, preferred_element_type=f32) + marks.astype(f32))[:1]
        at = (lax.broadcasted_iota(jnp.int32, (1, length), 1) + 1).astype(f32)
        prefix = rate * at + log_half * counted
        logs[...] = prefix
        total = counted[:, length - 1 :]
        closing = jnp.exp(rate * float(length) + log_half * total - prefix)
        share = fold(once(keys * closing, val, ((1,), (1,)))).astype(bf16)
        high = jnp.floor(total * (1.0 / COUNT_BASE))
        low = total - high * COUNT_BASE
        top = lax.broadcasted_iota(jnp.int32, (16, 2 * LANES), 0) == 0
        counts = jnp.where(top, high, low).astype(bf16)
        half = LANES // 2
        for z in range(payload.shape[0]):
            payload[z, :half] = share
            payload[z, half:] = counts
        masked = jnp.where(
            mask, thrice((keys * jnp.exp(-prefix)).T, recept * jnp.exp(prefix)), 0.0
        )
        scores[...] = masked.astype(bf16)
        own = jnp.sum(recept * (column(extra[...]) + 1.0) * keys, axis=0, keepdims=True)
        local[...] = thrice(val, masked) + own * val
        by_frame = tutor[...].astype(f32).T.astype(bf16)
        tiles = GRID["x"] * GRID["core"]
        part = length // tiles
        for i in range(tiles):
            held[i] = fold(by_frame[i * part : (i + 1) * part])
        place = lax.axis_index("x")
        for s, out in enumerate((t0, t1, t2, t3)):
            to = lax.rem(place + s, GRID["x"])
            out[...] = jnp.concatenate([beside(held[to * 2 + c]) for c in range(2)], axis=1)


def decays(everyone, rate, z, length):
    half = LANES // 2
    total = everyone[z, half : half + 1].astype(f32) * COUNT_BASE + everyone[
        z, half + 1 : half + 2
    ].astype(f32)
    return jnp.exp(rate * float(length) + log_half * total)


def folded_rates(codes_row, all_frames):
    return fold(jnp.broadcast_to(rates(codes_row, all_frames), (LANES, LANES)))


def yields_kernel(all_frames, everyone, local, reads, logs, codes, gain, sent, start, unit, inverse):
    length = local.shape[1]
    mine = lax.axis_index("ctx")
    half = LANES // 2
    rate = folded_rates(codes[...], all_frames)
    state = jnp.zeros((half, 2 * LANES), f32)
    for z in range(everyone.shape[0] - 1):
        longer = decays(everyone, rate, z, length) * state + everyone[z, :half].astype(f32)
        state = jnp.where(z < mine, longer, state)
    begin = unfold(state)
    start[...] = begin
    y = local[...] + thrice(begin.T, reads[...] * jnp.exp(logs[...]))
    centred = y - over_channels(y)
    inv = lax.rsqrt(over_channels(centred * centred) + epsilon)
    inverse[...] = inv
    unit[...] = centred * inv
    normed = (centred * inv * column(gain[...])).T.astype(bf16)
    tiles = GRID["x"] * GRID["core"]
    part = length // tiles
    for i in range(tiles):
        block = fold(normed[i * part : (i + 1) * part])
        for j in range(GRID["y"]):
            sent[j * tiles + i] = block


def spread(blocks):
    cols = []
    for a, b in zip(blocks[::2], blocks[1::2]):
        cols.append(
            jnp.concatenate(
                [
                    jnp.concatenate([a[:, :LANES], b[:, :LANES]], axis=1),
                    jnp.concatenate([a[:, LANES:], b[:, LANES:]], axis=1),
                ],
                axis=0,
            )
        )
    return jnp.concatenate(cols, axis=1)


def pack_kernel(columns, t0, t1, t2, t3, p0, p1, p2, p3):
    rows = columns.shape[0] * columns.shape[1]
    matrix = columns[...].reshape(rows, columns.shape[2])
    for out, teacher in ((p0, t0), (p1, t1), (p2, t2), (p3, t3)):
        out[:rows] = matrix
        out[rows:] = teacher[...]


def by_source(mine, other, x, c):
    step = lax.rem(lax.axis_index("x") - x + GRID["x"], GRID["x"])
    core = lax.axis_index("core")
    return jnp.where(core == c, mine[step, core], other[step, core])


def middle_kernel(got, w0, w3, w2, w1, v0, v3, v2, v1, sent, m0, m1, m2, m3, held, weights, sems):
    copies = []
    for n, source in enumerate((w0, v0, w1, v1, w2, v2, w3, v3)):
        copies.append(pltpu.make_async_copy(source, weights.at[n], sems.at[n]))
        copies[n].start()
    at, core = lax.axis_index("x"), lax.axis_index("core")
    tiles = GRID["x"] * GRID["core"]
    rows = GRID["y"]
    group = min(4, rows)
    chunks = []
    for s in (0, 3, 2, 1):
        x = lax.rem(at - s + GRID["x"], GRID["x"])
        for n, c in ((2 * s, core), (2 * s + 1, 1 - core)):
            for y in range(0, rows, group):
                chunks.append((n, y, [(y + g) * tiles + x * 2 + c for g in range(group)]))
    acc = None
    for n, y, places in chunks:
        if y == 0:
            copies[n].wait()
        part = weights[n, y * LANES : (y + group) * LANES]
        term = jnp.dot(spread([got[p] for p in places]), part, preferred_element_type=f32)
        acc = term if acc is None else acc + term
    mixed = acc.astype(bf16)
    for i in range(tiles):
        held[i] = fold(mixed[:, i * LANES : (i + 1) * LANES])
    for s, out in enumerate((m0, m1, m2, m3)):
        to = lax.rem(at + s, GRID["x"])
        for c in range(2):
            out[c] = held[to * 2 + c]
    teachers = []
    for i in range(tiles):
        step = lax.rem(at - i // 2 + GRID["x"], GRID["x"])
        came = weights[2 * step + jnp.where(core == i % 2, 0, 1), rows * LANES :]
        wide = came.shape[1] // 2
        mine = jnp.where(core == 0, came[:, :wide], came[:, wide:])
        teachers.append(jnp.concatenate([mine[:, : wide // 2], mine[:, wide // 2 :]], axis=0))
    wanted = spread(teachers)
    diff = (mixed.astype(f32) - wanted.astype(f32)).astype(bf16)
    for n, y, places in chunks:
        part = weights[n, y * LANES : (y + group) * LANES]
        grads = lax.dot_general(
            part, diff, (((1,), (1,)), ((), ())), preferred_element_type=f32
        ).astype(bf16)
        for g, p in enumerate(places):
            sent[p] = fold(grads[g * LANES : (g + 1) * LANES])


def back_kernel(got, unit, inverse, gain, reads, logs, payload, sensitivity):
    tiles = GRID["x"] * GRID["core"]
    frames = []
    for i in range(tiles):
        total = got[i].astype(f32)
        for j in range(1, GRID["y"]):
            total = total + got[j * tiles + i].astype(f32)
        frames.append(unfold(total))
    scaled = jnp.concatenate(frames, axis=1) * column(gain[...])
    each = unit[...]
    grad = inverse[...] * (
        scaled - over_channels(scaled) - each * over_channels(scaled * each)
    )
    sensitivity[...] = grad
    share = fold(once(reads[...] * jnp.exp(logs[...]), grad, ((1,), (1,)))).astype(bf16)
    for z in range(payload.shape[0]):
        payload[z] = share


def window_kernel(
    m_mine, m_other, reads, keys_raw, values, logs, extra, scores, start, sensitivity,
    mixed_out, grad_reads, part_keys, part_values,
):
    length = reads.shape[1]
    tiles = GRID["x"] * GRID["core"]
    mixed_out[...] = (
        jnp.concatenate(
            [
                unfold(by_source(m_mine, m_other, i // 2, i % 2).astype(f32))
                for i in range(tiles)
            ],
            axis=0,
        ).T.astype(bf16)
    )
    recept, val, grad = reads[...], values[...], sensitivity[...]
    keys, _ = key_norm(keys_raw[...])
    prefix = logs[...]
    grow, shrink = jnp.exp(prefix), jnp.exp(-prefix)
    own_weight = column(extra[...]) + 1.0
    twofold = jnp.where(earlier(length), once(val.T, grad, ((1,), (0,))), 0.0).astype(bf16)
    progressive = jnp.sum(grad * val, axis=0, keepdims=True) * own_weight
    own = jnp.sum(recept * own_weight * keys, axis=0, keepdims=True)
    grad_reads[...] = (
        grow * (once(start[...], grad, ((1,), (0,))) + once(keys * shrink, twofold, ((1,), (0,)))) + progressive * keys
    ).astype(bf16)
    part_keys[...] = shrink * once(recept * grow, twofold, ((1,), (1,))) + progressive * recept
    part_values[...] = once(grad, scores[...], ((1,), (1,))) + own * grad


def final_kernel(
    all_frames, later, everyone, part_keys, part_values, keys_raw, values, logs, codes,
    grad_keys, grad_values,
):
    length = keys_raw.shape[1]
    mine = lax.axis_index("ctx")
    half = LANES // 2
    rate = folded_rates(codes[...], all_frames)
    state = jnp.zeros((half, 2 * LANES), f32)
    for z in range(everyone.shape[0] - 1, 0, -1):
        longer = decays(everyone, rate, z, length) * state + later[z].astype(f32)
        state = jnp.where(z > mine, longer, state)
    walking = unfold(state)
    raw = keys_raw[...]
    keys, scale = key_norm(raw)
    prefix = logs[...]
    closing = jnp.exp(prefix[:, length - 1 :] - prefix)
    grad = part_keys[...] + closing * once(walking, values[...], ((1,), (0,)))
    grad_values[...] = (part_values[...] + once(walking.T, keys * closing, ((1,), (0,)))).astype(bf16)
    grad_keys[...] = (
        0.125 * scale * (grad - scale * scale * raw * over_channels(raw * grad))
    ).astype(bf16)


def call(kernel, outs, args, here=(), cost=1 << 23, **more):
    return pl.pallas_call(
        kernel,
        cost_estimate=pl.CostEstimate(flops=1 << 30, transcendentals=0, bytes_accessed=cost),
        out_shape=[
            pltpu.VMEM(shape, kind) if n in here else jax.ShapeDtypeStruct(shape, kind)
            for n, (shape, kind) in enumerate(outs)
        ],
        **more,
    )(*args)


def near(*arrays):
    return tuple(pltpu.with_memory_space_constraint(a, pltpu.VMEM) for a in arrays)


def exchange(array, axis):
    return lax.all_to_all(array, axis, 0, 0)


def along_x(parts):
    n = GRID["x"]
    came = {
        s: lax.ppermute(parts[s], "x", [(i, (i + s) % n) for i in range(n)]) for s in (3, 2, 1)
    }
    return [parts[0], came[1], came[2], came[3]]


def swap(array):
    return lax.ppermute(array, "core", [(0, 1), (1, 0)])


def on_device(
    incoming_signals,
    receptor_linear_map,
    lock_linear_map,
    worth_linear_map,
    outbound_linear_map,
    selfward_extra,
    cluster_amplify_level,
    dwindle_powers,
    bisect_indicators,
    tutor_aggregated,
):
    length, width = incoming_signals.shape
    blocks = lax.axis_size("ctx")
    tiles, rows = GRID["x"] * GRID["core"], GRID["y"]
    part = length // tiles
    all_frames = length * blocks
    half = LANES // 2
    head = tuple(GRID)
    flat = (LANES, length)
    block = (part // 2, 2 * LANES)
    teacher = ((part // 4, 8 * LANES), bf16)
    barrier = lax.optimization_barrier

    columns = exchange(
        outbound_linear_map.reshape(LANES, rows, tiles * LANES).transpose(1, 0, 2), "y"
    )

    codes = dwindle_powers.reshape(1, LANES)
    extra = selfward_extra.reshape(1, LANES)
    gain = cluster_amplify_level.reshape(1, LANES)
    halvings = bisect_indicators.reshape(1, length)

    depth = width // STEPS
    whole = pl.BlockSpec(memory_space=pltpu.VMEM)
    by_step = [
        pl.BlockSpec((length, depth), lambda k: (0, k)),
        pl.BlockSpec((LANES, depth), lambda k: (0, k)),
    ]
    payload, reads, keys_raw, values, logs, scores, local, *tutor = call(
        functools.partial(project_kernel, all_frames),
        [
            ((blocks, half + 16, 2 * LANES), bf16), (flat, f32), (flat, f32), (flat, f32),
            (flat, f32), ((length, length), bf16), (flat, f32),
        ]
        + [teacher] * GRID["x"],
        (
            incoming_signals, receptor_linear_map.T, lock_linear_map.T, worth_linear_map.T,
            codes, halvings, extra, tutor_aggregated.T,
        ),
        here=(1, 4, 6),
        grid=(STEPS,),
        in_specs=[by_step[0]] + [by_step[1]] * 3 + [whole] * 4,
        out_specs=[whole] * (7 + GRID["x"]),
        scratch_shapes=[
            pltpu.VMEM((length, 3 * LANES), f32), pltpu.VMEM((tiles,) + block, bf16),
        ],
    )
    payload, columns, *tutor = barrier((payload, columns, *tutor))
    everyone = exchange(payload, "ctx")
    packed = call(
        pack_kernel,
        [((rows * LANES + teacher[0][0], tiles * LANES), bf16)] * GRID["x"],
        near(columns) + tuple(tutor),
    )
    w_mine = along_x(packed)
    sent, start, unit, inverse = call(
        functools.partial(yields_kernel, all_frames),
        [((rows * tiles,) + block, bf16), ((LANES, LANES), f32), (flat, f32), ((1, length), f32)],
        near(everyone, local, reads, logs) + (codes, gain),
        here=(2, 3),
    )
    got = exchange(sent, head)
    other = {s: swap(w_mine[s]) for s in (0, 3, 2, 1)}
    w_other = [other[s] for s in (0, 3, 2, 1)]
    w_mine = [w_mine[s] for s in (0, 3, 2, 1)]
    sent, *mixed = call(
        middle_kernel,
        [((rows * tiles,) + block, bf16)] + [((2,) + block, bf16)] * GRID["x"],
        near(got) + (*w_mine,) + near(w_other[0]) + (*w_other[1:],),
        in_specs=[whole]
        + [pl.BlockSpec(memory_space=pl.ANY)] * GRID["x"]
        + [whole]
        + [pl.BlockSpec(memory_space=pl.ANY)] * (GRID["x"] - 1),
        scratch_shapes=[
            pltpu.VMEM((tiles,) + block, bf16),
            pltpu.VMEM((2 * GRID["x"],) + packed[0].shape, bf16),
            pltpu.SemaphoreType.DMA((2 * GRID["x"],)),
        ],
    )
    got = exchange(sent, head)
    mixed = jnp.stack(along_x(mixed))
    payload, sensitivity = call(
        back_kernel,
        [((blocks, half, 2 * LANES), bf16), (flat, f32)],
        near(got, unit, inverse) + (gain,) + near(reads, logs),
    )
    later = exchange(payload, "ctx")
    mixed_out, grad_reads, part_keys, part_values = call(
        window_kernel,
        [(flat, bf16), (flat, bf16), (flat, f32), (flat, f32)],
        (mixed, swap(mixed), reads, keys_raw, values, logs, extra, scores, start, sensitivity),
        here=(2, 3),
    )
    grad_keys, grad_values = call(
        functools.partial(final_kernel, all_frames),
        [(flat, bf16), (flat, bf16)],
        near(later, everyone, part_keys, part_values, keys_raw, values, logs) + (codes,),
    )
    return (mixed_out.T, grad_reads.T, grad_keys.T, grad_values.T)


def solution(mesh):
    blocks = mesh.shape["ctx"]
    grid = Mesh(mesh.devices.reshape((blocks,) + tuple(GRID.values())), ("ctx",) + tuple(GRID))
    head = tuple(GRID)
    in_specs = (
        P("ctx", None),
        P(None, head),
        P(None, head),
        P(None, head),
        P(head, None),
        P(head),
        P(head),
        P(head),
        P("ctx"),
        P("ctx", head),
    )
    out_specs = (P("ctx", head), P("ctx", head), P("ctx", head), P("ctx", head))
    return jax.shard_map(
        on_device, mesh=grid, in_specs=in_specs, out_specs=out_specs, check_vma=False
    )
```

```python
import functools

import jax
import jax.numpy as jnp
from jax import lax
from jax.experimental import pallas as pl
from jax.experimental.pallas import tpu as pltpu
from jax.sharding import Mesh, PartitionSpec as P

LANES = 64
CODES = 64
GRID = {"y": 8, "x": 4, "core": 2}
STEPS = 4
COUNT_BASE = 64

epsilon = 1e-05
log_half = -0.6931471805599453
rate_span = 1.2
f32 = jnp.float32
bf16 = jnp.bfloat16


def once(a, b, dims):
    return lax.dot_general(
        a.astype(bf16), b.astype(bf16), (dims, ((), ())), preferred_element_type=f32
    )


def split(a):
    high = a.astype(bf16)
    return high, (a - high.astype(f32)).astype(bf16)


def thrice(a, b):
    (a_high, a_low), (b_high, b_low) = split(a), split(b)
    if a.shape[1] <= LANES:
        return once(
            jnp.concatenate([a_high, a_high, a_low], axis=1),
            jnp.concatenate([b_high, b_low, b_high], axis=0),
            ((1,), (0,)),
        )
    both = once(jnp.concatenate([a_high, a_low], axis=0), b_high, ((1,), (0,)))
    rows = a.shape[0]
    return both[:rows] + both[rows:] + once(a_high, b_low, ((1,), (0,)))


def column(row):
    n = row.shape[1]
    at = lax.broadcasted_iota(jnp.int32, (n, n), 0)
    on = at == lax.broadcasted_iota(jnp.int32, (n, n), 1)
    return jnp.sum(jnp.where(on, row, 0.0), axis=1, keepdims=True)


def rates(codes_row, all_frames):
    return -rate_span * (column(codes_row.astype(f32)) + 1.0) / float(CODES * all_frames)


def over_channels(array):
    return jnp.mean(array, axis=0, keepdims=True)


def key_norm(keys_raw):
    scale = lax.rsqrt(over_channels(keys_raw * keys_raw) + epsilon)
    return keys_raw * scale * 0.125, scale


def fold(square):
    half = square.shape[0] // 2
    return jnp.concatenate([square[:half], square[half:]], axis=1)


def beside(block):
    half = block.shape[0] // 2
    return jnp.concatenate([block[:half], block[half:]], axis=1)


def unfold(packed):
    return jnp.concatenate([packed[:, :LANES], packed[:, LANES:]], axis=0)


def earlier(length):
    s = lax.broadcasted_iota(jnp.int32, (length, length), 0)
    return s < lax.broadcasted_iota(jnp.int32, (length, length), 1)


def project_kernel(
    all_frames, x, wr, wk, wv, codes, halvings, extra, tutor,
    payload, reads, keys_raw, values, logs, scores, local, t0, t1, t2, t3, acc, held,
):
    step = pl.program_id(0)

    @pl.when(step == 0)
    def _():
        acc[...] = jnp.zeros_like(acc)

    acc[...] += lax.dot_general(
        x[...],
        jnp.concatenate([wr[...], wk[...], wv[...]], axis=0),
        (((1,), (1,)), ((), ())),
        preferred_element_type=f32,
    )

    @pl.when(step == STEPS - 1)
    def _():
        length = x.shape[0]
        whole = acc[...].T
        recept, raw, val = whole[:LANES], whole[LANES : 2 * LANES], whole[2 * LANES :]
        reads[...] = recept
        keys_raw[...] = raw
        values[...] = val
        keys, _ = key_norm(raw)
        rate = rates(codes[...], all_frames)
        marks = jnp.broadcast_to(halvings[...].astype(f32).astype(bf16), (16, length))
        mask = earlier(length)
        ones = jnp.where(mask, 1.0, 0.0).astype(bf16)
        counted = (jnp.dot(marks, ones, preferred_element_type=f32) + marks.astype(f32))[:1]
        at = (lax.broadcasted_iota(jnp.int32, (1, length), 1) + 1).astype(f32)
        prefix = rate * at + log_half * counted
        logs[...] = prefix
        total = counted[:, length - 1 :]
        closing = jnp.exp(rate * float(length) + log_half * total - prefix)
        share = fold(once(keys * closing, val, ((1,), (1,)))).astype(bf16)
        high = jnp.floor(total * (1.0 / COUNT_BASE))
        low = total - high * COUNT_BASE
        top = lax.broadcasted_iota(jnp.int32, (16, 2 * LANES), 0) == 0
        counts = jnp.where(top, high, low).astype(bf16)
        half = LANES // 2
        for z in range(payload.shape[0]):
            payload[z, :half] = share
            payload[z, half:] = counts
        masked = jnp.where(
            mask, thrice((keys * jnp.exp(-prefix)).T, recept * jnp.exp(prefix)), 0.0
        )
        scores[...] = masked.astype(bf16)
        own = jnp.sum(recept * (column(extra[...]) + 1.0) * keys, axis=0, keepdims=True)
        local[...] = thrice(val, masked) + own * val
        by_frame = tutor[...].astype(f32).T.astype(bf16)
        tiles = GRID["x"] * GRID["core"]
        part = length // tiles
        for i in range(tiles):
            held[i] = fold(by_frame[i * part : (i + 1) * part])
        place = lax.axis_index("x")
        for s, out in enumerate((t0, t1, t2, t3)):
            to = lax.rem(place + s, GRID["x"])
            out[...] = jnp.concatenate([beside(held[to * 2 + c]) for c in range(2)], axis=1)


def decays(everyone, rate, z, length):
    half = LANES // 2
    total = everyone[z, half : half + 1].astype(f32) * COUNT_BASE + everyone[
        z, half + 1 : half + 2
    ].astype(f32)
    return jnp.exp(rate * float(length) + log_half * total)


def folded_rates(codes_row, all_frames):
    return fold(jnp.broadcast_to(rates(codes_row, all_frames), (LANES, LANES)))


def yields_kernel(all_frames, everyone, local, reads, logs, codes, gain, sent, start, unit, inverse):
    length = local.shape[1]
    mine = lax.axis_index("ctx")
    half = LANES // 2
    rate = folded_rates(codes[...], all_frames)
    state = jnp.zeros((half, 2 * LANES), f32)
    for z in range(everyone.shape[0] - 1):
        longer = decays(everyone, rate, z, length) * state + everyone[z, :half].astype(f32)
        state = jnp.where(z < mine, longer, state)
    begin = unfold(state)
    start[...] = begin
    y = local[...] + thrice(begin.T, reads[...] * jnp.exp(logs[...]))
    centred = y - over_channels(y)
    inv = lax.rsqrt(over_channels(centred * centred) + epsilon)
    inverse[...] = inv
    unit[...] = centred * inv
    normed = (centred * inv * column(gain[...])).T.astype(bf16)
    tiles = GRID["x"] * GRID["core"]
    part = length // tiles
    for i in range(tiles):
        block = fold(normed[i * part : (i + 1) * part])
        for j in range(GRID["y"]):
            sent[j * tiles + i] = block


def spread(blocks):
    cols = []
    for a, b in zip(blocks[::2], blocks[1::2]):
        cols.append(
            jnp.concatenate(
                [
                    jnp.concatenate([a[:, :LANES], b[:, :LANES]], axis=1),
                    jnp.concatenate([a[:, LANES:], b[:, LANES:]], axis=1),
                ],
                axis=0,
            )
        )
    return jnp.concatenate(cols, axis=1)


def pack_kernel(columns, t0, t1, t2, t3, p0, p1, p2, p3):
    rows = columns.shape[0] * columns.shape[1]
    matrix = columns[...].reshape(rows, columns.shape[2])
    for out, teacher in ((p0, t0), (p1, t1), (p2, t2), (p3, t3)):
        out[:rows] = matrix
        out[rows:] = teacher[...]


def by_source(mine, other, x, c):
    step = lax.rem(lax.axis_index("x") - x + GRID["x"], GRID["x"])
    core = lax.axis_index("core")
    return jnp.where(core == c, mine[step, core], other[step, core])


def middle_kernel(got, w0, w1, w2, w3, v0, v1, v2, v3, sent, m0, m1, m2, m3, held, weights, sems):
    copies = []
    for n, source in enumerate((w0, v0, w1, v1, w2, v2, w3, v3)):
        copies.append(pltpu.make_async_copy(source, weights.at[n], sems.at[n]))
        copies[n].start()
    at, core = lax.axis_index("x"), lax.axis_index("core")
    tiles = GRID["x"] * GRID["core"]
    rows = GRID["y"]
    group = min(4, rows)
    chunks = []
    for s in (0, 1, 2, 3):
        x = lax.rem(at - s + GRID["x"], GRID["x"])
        for n, c in ((2 * s, core), (2 * s + 1, 1 - core)):
            for y in range(0, rows, group):
                chunks.append((n, y, [(y + g) * tiles + x * 2 + c for g in range(group)]))
    acc = None
    for n, y, places in chunks:
        if y == 0:
            copies[n].wait()
        part = weights[n, y * LANES : (y + group) * LANES]
        term = jnp.dot(spread([got[p] for p in places]), part, preferred_element_type=f32)
        acc = term if acc is None else acc + term
    mixed = acc.astype(bf16)
    for i in range(tiles):
        held[i] = fold(mixed[:, i * LANES : (i + 1) * LANES])
    for s, out in enumerate((m0, m1, m2, m3)):
        to = lax.rem(at + s, GRID["x"])
        for c in range(2):
            out[c] = held[to * 2 + c]
    teachers = []
    for i in range(tiles):
        step = lax.rem(at - i // 2 + GRID["x"], GRID["x"])
        came = weights[2 * step + jnp.where(core == i % 2, 0, 1), rows * LANES :]
        wide = came.shape[1] // 2
        mine = jnp.where(core == 0, came[:, :wide], came[:, wide:])
        teachers.append(jnp.concatenate([mine[:, : wide // 2], mine[:, wide // 2 :]], axis=0))
    wanted = spread(teachers)
    diff = (mixed.astype(f32) - wanted.astype(f32)).astype(bf16)
    for n, y, places in chunks:
        part = weights[n, y * LANES : (y + group) * LANES]
        grads = lax.dot_general(
            part, diff, (((1,), (1,)), ((), ())), preferred_element_type=f32
        ).astype(bf16)
        for g, p in enumerate(places):
            sent[p] = fold(grads[g * LANES : (g + 1) * LANES])


def back_kernel(got, unit, inverse, gain, reads, logs, payload, sensitivity):
    tiles = GRID["x"] * GRID["core"]
    frames = []
    for i in range(tiles):
        total = got[i].astype(f32)
        for j in range(1, GRID["y"]):
            total = total + got[j * tiles + i].astype(f32)
        frames.append(unfold(total))
    scaled = jnp.concatenate(frames, axis=1) * column(gain[...])
    each = unit[...]
    grad = inverse[...] * (
        scaled - over_channels(scaled) - each * over_channels(scaled * each)
    )
    sensitivity[...] = grad
    share = fold(once(reads[...] * jnp.exp(logs[...]), grad, ((1,), (1,)))).astype(bf16)
    for z in range(payload.shape[0]):
        payload[z] = share


def window_kernel(
    m_mine, m_other, reads, keys_raw, values, logs, extra, scores, start, sensitivity,
    mixed_out, grad_reads, part_keys, part_values,
):
    length = reads.shape[1]
    tiles = GRID["x"] * GRID["core"]
    mixed_out[...] = (
        jnp.concatenate(
            [
                unfold(by_source(m_mine, m_other, i // 2, i % 2).astype(f32))
                for i in range(tiles)
            ],
            axis=0,
        ).T.astype(bf16)
    )
    recept, val, grad = reads[...], values[...], sensitivity[...]
    keys, _ = key_norm(keys_raw[...])
    prefix = logs[...]
    grow, shrink = jnp.exp(prefix), jnp.exp(-prefix)
    own_weight = column(extra[...]) + 1.0
    twofold = jnp.where(earlier(length), once(val.T, grad, ((1,), (0,))), 0.0).astype(bf16)
    progressive = jnp.sum(grad * val, axis=0, keepdims=True) * own_weight
    own = jnp.sum(recept * own_weight * keys, axis=0, keepdims=True)
    grad_reads[...] = (
        grow * (once(start[...], grad, ((1,), (0,))) + once(keys * shrink, twofold, ((1,), (0,)))) + progressive * keys
    ).astype(bf16)
    part_keys[...] = shrink * once(recept * grow, twofold, ((1,), (1,))) + progressive * recept
    part_values[...] = once(grad, scores[...], ((1,), (1,))) + own * grad


def final_kernel(
    all_frames, later, everyone, part_keys, part_values, keys_raw, values, logs, codes,
    grad_keys, grad_values,
):
    length = keys_raw.shape[1]
    mine = lax.axis_index("ctx")
    half = LANES // 2
    rate = folded_rates(codes[...], all_frames)
    state = jnp.zeros((half, 2 * LANES), f32)
    for z in range(everyone.shape[0] - 1, 0, -1):
        longer = decays(everyone, rate, z, length) * state + later[z].astype(f32)
        state = jnp.where(z > mine, longer, state)
    walking = unfold(state)
    raw = keys_raw[...]
    keys, scale = key_norm(raw)
    prefix = logs[...]
    closing = jnp.exp(prefix[:, length - 1 :] - prefix)
    grad = part_keys[...] + closing * once(walking, values[...], ((1,), (0,)))
    grad_values[...] = (part_values[...] + once(walking.T, keys * closing, ((1,), (0,)))).astype(bf16)
    grad_keys[...] = (
        0.125 * scale * (grad - scale * scale * raw * over_channels(raw * grad))
    ).astype(bf16)


def call(kernel, outs, args, here=(), cost=1 << 23, **more):
    return pl.pallas_call(
        kernel,
        cost_estimate=pl.CostEstimate(flops=1 << 30, transcendentals=0, bytes_accessed=cost),
        out_shape=[
            pltpu.VMEM(shape, kind) if n in here else jax.ShapeDtypeStruct(shape, kind)
            for n, (shape, kind) in enumerate(outs)
        ],
        **more,
    )(*args)


def near(*arrays):
    return tuple(pltpu.with_memory_space_constraint(a, pltpu.VMEM) for a in arrays)


def exchange(array, axis):
    return lax.all_to_all(array, axis, 0, 0)


def along_x(parts):
    n = GRID["x"]
    came = {
        s: lax.ppermute(parts[s], "x", [(i, (i + s) % n) for i in range(n)]) for s in (1, 2, 3)
    }
    return [parts[0], came[1], came[2], came[3]]


def swap(array):
    return lax.ppermute(array, "core", [(0, 1), (1, 0)])


def on_device(
    incoming_signals,
    receptor_linear_map,
    lock_linear_map,
    worth_linear_map,
    outbound_linear_map,
    selfward_extra,
    cluster_amplify_level,
    dwindle_powers,
    bisect_indicators,
    tutor_aggregated,
):
    length, width = incoming_signals.shape
    blocks = lax.axis_size("ctx")
    tiles, rows = GRID["x"] * GRID["core"], GRID["y"]
    part = length // tiles
    all_frames = length * blocks
    half = LANES // 2
    head = tuple(GRID)
    flat = (LANES, length)
    block = (part // 2, 2 * LANES)
    teacher = ((part // 4, 8 * LANES), bf16)
    barrier = lax.optimization_barrier

    columns = exchange(
        outbound_linear_map.reshape(LANES, rows, tiles * LANES).transpose(1, 0, 2), "y"
    )

    codes = dwindle_powers.reshape(1, LANES)
    extra = selfward_extra.reshape(1, LANES)
    gain = cluster_amplify_level.reshape(1, LANES)
    halvings = bisect_indicators.reshape(1, length)

    depth = width // STEPS
    whole = pl.BlockSpec(memory_space=pltpu.VMEM)
    by_step = [
        pl.BlockSpec((length, depth), lambda k: (0, k)),
        pl.BlockSpec((LANES, depth), lambda k: (0, k)),
    ]
    payload, reads, keys_raw, values, logs, scores, local, *tutor = call(
        functools.partial(project_kernel, all_frames),
        [
            ((blocks, half + 16, 2 * LANES), bf16), (flat, f32), (flat, f32), (flat, f32),
            (flat, f32), ((length, length), bf16), (flat, f32),
        ]
        + [teacher] * GRID["x"],
        (
            incoming_signals, receptor_linear_map.T, lock_linear_map.T, worth_linear_map.T,
            codes, halvings, extra, tutor_aggregated.T,
        ),
        here=(1, 4, 6),
        grid=(STEPS,),
        in_specs=[by_step[0]] + [by_step[1]] * 3 + [whole] * 4,
        out_specs=[whole] * (7 + GRID["x"]),
        scratch_shapes=[
            pltpu.VMEM((length, 3 * LANES), f32), pltpu.VMEM((tiles,) + block, bf16),
        ],
    )
    payload, columns, *tutor = barrier((payload, columns, *tutor))
    everyone = exchange(payload, "ctx")
    packed = call(
        pack_kernel,
        [((rows * LANES + teacher[0][0], tiles * LANES), bf16)] * GRID["x"],
        near(columns) + tuple(tutor),
    )
    w_mine = along_x(packed)
    sent, start, unit, inverse = call(
        functools.partial(yields_kernel, all_frames),
        [((rows * tiles,) + block, bf16), ((LANES, LANES), f32), (flat, f32), ((1, length), f32)],
        near(everyone, local, reads, logs) + (codes, gain),
        here=(2, 3),
    )
    got = exchange(sent, head)
    other = {s: swap(w_mine[s]) for s in (0, 1, 2, 3)}
    w_other = [other[s] for s in (0, 1, 2, 3)]
    w_mine = [w_mine[s] for s in (0, 1, 2, 3)]
    sent, *mixed = call(
        middle_kernel,
        [((rows * tiles,) + block, bf16)] + [((2,) + block, bf16)] * GRID["x"],
        near(got) + (*w_mine,) + near(w_other[0]) + (*w_other[1:],),
        in_specs=[whole]
        + [pl.BlockSpec(memory_space=pl.ANY)] * GRID["x"]
        + [whole]
        + [pl.BlockSpec(memory_space=pl.ANY)] * (GRID["x"] - 1),
        scratch_shapes=[
            pltpu.VMEM((tiles,) + block, bf16),
            pltpu.VMEM((2 * GRID["x"],) + packed[0].shape, bf16),
            pltpu.SemaphoreType.DMA((2 * GRID["x"],)),
        ],
    )
    got = exchange(sent, head)
    mixed = jnp.stack(along_x(mixed))
    payload, sensitivity = call(
        back_kernel,
        [((blocks, half, 2 * LANES), bf16), (flat, f32)],
        near(got, unit, inverse) + (gain,) + near(reads, logs),
    )
    later = exchange(payload, "ctx")
    mixed_out, grad_reads, part_keys, part_values = call(
        window_kernel,
        [(flat, bf16), (flat, bf16), (flat, f32), (flat, f32)],
        (mixed, swap(mixed), reads, keys_raw, values, logs, extra, scores, start, sensitivity),
        here=(2, 3),
    )
    grad_keys, grad_values = call(
        functools.partial(final_kernel, all_frames),
        [(flat, bf16), (flat, bf16)],
        near(later, everyone, part_keys, part_values, keys_raw, values, logs) + (codes,),
    )
    return (mixed_out.T, grad_reads.T, grad_keys.T, grad_values.T)


def solution(mesh):
    blocks = mesh.shape["ctx"]
    grid = Mesh(mesh.devices.reshape((blocks,) + tuple(GRID.values())), ("ctx",) + tuple(GRID))
    head = tuple(GRID)
    in_specs = (
        P("ctx", None),
        P(None, head),
        P(None, head),
        P(None, head),
        P(head, None),
        P(head),
        P(head),
        P(head),
        P("ctx"),
        P("ctx", head),
    )
    out_specs = (P("ctx", head), P("ctx", head), P("ctx", head), P("ctx", head))
    return jax.shard_map(
        on_device, mesh=grid, in_specs=in_specs, out_specs=out_specs, check_vma=False
    )
```
